32 devices in a mesh: groups: 2 (over y), tm: 8 (over z, x), head: 2 (over core).
Axes of the slice: x: 2, y: 2, z: 4, core: 2. Of those that a mesh axis runs over, the one named last changes fastest.
Arguments:
- queries: bfloat16 [1536, 2560], P(('groups', 'tm'), 'head'), parts along dimension 0, may hold values from -1000 to 1000
- keys: bfloat16 [1536, 2560], P(('groups', 'tm'), 'head'), parts along dimension 0, may hold values from -1000 to 1000
- values: bfloat16 [1536, 2560], P(('groups', 'tm'), 'head'), parts along dimension 0, may hold values from -6 to 6
- q_gain: float32 [2560], P('head'), may hold values from 1 to 2
- k_gain: float32 [2560], P('head'), may hold values from 1 to 2
- frames: int32 [16], P(('groups', 'tm')), parts along dimension 0, may hold values from 1 to 3
- flags: int32 [16, 2], P(('groups', 'tm')), parts along dimension 0, may hold values 0 or 1
Outputs:
- attended: bfloat16 [1536, 2560], P(('groups', 'tm'), 'head'), parts along dimension 0
The draws below stay inside these ranges and needn't reach their ends.
There are 2 independent parts, one for each index of `groups`. The reference program is written for one: setup_inputs(seed, part) draws one part's arguments, and reference() takes and returns one part's arrays. A program takes and returns all parts, laid end to end along the dimension named above; an argument that names none is the same for every part. Nothing has to cross between parts.
All inputs are finite; a program needn't handle non-finite values. No bound on the sum of `flags` on one device may be relied on, other than what follows from the above.
Results may differ from the reference program's by a relative error of at most 0.011.
Values may be sent and summed in bfloat16 or wider, within the bound.
No kernel may reach another device: no remote copies, remote signals or barrier semaphores. Data moves between devices by JAX's collectives and lax.ppermute only.
A program may use at most 128 MiB of HBM per device.

```python
import math
import jax
import jax.numpy as jnp
from jax import lax

HD = 128
HEADS = 20
FT = 32
F_C = 3
COLS = 2560
T_C = 96
WIN = 64
SPANS = 8
TOKENS = 768


def query_key_fields(key):
    parts = jax.random.split(key, 6)
    tilt = math.sqrt(3.0)
    column_index = jnp.arange(COLS)
    upper_half = jnp.where(column_index >= COLS // 2, tilt, 1.0)
    row_top = 10.0

    def one_field(noise_key, row_key, column_key):
        base = jnp.clip(jax.random.normal(noise_key, (TOKENS, COLS)), -4.0, 4.0)
        row_scale = jnp.exp(jax.random.uniform(row_key, (TOKENS, 1)) * math.log(row_top))
        column_scale = jnp.exp(jax.random.uniform(column_key, (1, COLS)) * math.log(10.0))
        return base * row_scale * column_scale * upper_half[None, :]
    query_field = one_field(parts[0], parts[2], parts[4])
    key_field = one_field(parts[1], parts[3], parts[5])
    return (query_field, key_field)


def draw_queries(key, part):
    return query_key_fields(key)[0].astype(jnp.bfloat16)


def draw_keys(key, part):
    return query_key_fields(key)[1].astype(jnp.bfloat16)


def plant(values, key, least, largest):
    dims = values.shape
    spot = [jax.random.randint(jax.random.fold_in(key, axis), (), 0, dims[axis]) for axis in range(len(dims))]
    values = values.at[tuple(spot)].set(least)
    longest = dims.index(max(dims))
    spot[longest] = (spot[longest] + 1) % dims[longest]
    return values.at[tuple(spot)].set(largest)


def steps_of(own_key, shape, cuts, least, largest):
    level = 1.0
    for position, blocks in cuts:
        steps = jax.random.uniform(jax.random.fold_in(jax.random.fold_in(own_key, 6), position), (blocks,), jnp.float32, least / len(cuts), largest / len(cuts))
        level = level * jnp.repeat(jnp.exp(steps), shape[position] // blocks).reshape((-1,) + (1,) * (len(shape) - 1 - position))
    return level


def gaussian(key, dims, deviation, limit, shards=(), kind=jnp.bfloat16):
    values = deviation * jax.random.normal(key, dims, jnp.float32)
    if shards:
        values = values * steps_of(key, dims, shards, -0.22, 0.18)
    return jnp.clip(values, -limit, limit).astype(kind)


def setup_inputs(seed: int = 0, part: int = 0) -> dict:
    streams_of = jax.random.split(jax.random.key(seed), 8)
    part_splits = jax.random.split(jax.random.fold_in(streams_of[7], part), 8)
    return {
        "queries": draw_queries(jax.random.fold_in(jax.random.fold_in(streams_of[7], part), 71), part),
        "keys": draw_keys(jax.random.fold_in(jax.random.fold_in(streams_of[7], part), 71), part),
        "values": gaussian(part_splits[2], (TOKENS, COLS), 1.0, 6.0, ((0, 8), (1, 2))),
        "q_gain": jnp.clip(1.0 + 1.0 * jax.random.uniform(streams_of[3], (COLS,), jnp.float32) ** steps_of(streams_of[3], (COLS,), ((0, 2),), -0.2, 0.2), 1.0, 2.0),
        "k_gain": jnp.clip(1.0 + 1.0 * jax.random.uniform(streams_of[4], (COLS,), jnp.float32) ** steps_of(streams_of[4], (COLS,), ((0, 2),), -0.2, 0.2), 1.0, 2.0),
        "frames": plant(jax.random.randint(part_splits[5], (SPANS,), 1, F_C + 1), jax.random.fold_in(part_splits[5], 1), 1, F_C).astype(jnp.int32),
        "flags": plant((jax.random.randint(part_splits[6], (SPANS, 2), 0, 4) < 3).astype(jnp.int32), jax.random.fold_in(part_splits[6], 1), 0, 1),
    }


EPSILON = 1e-06

def rms_rows(inputs, gain):
    widened = inputs.astype(jnp.float32)
    level = lax.optimization_barrier(jnp.mean(widened * widened, axis=1, keepdims=True))
    return (widened * lax.rsqrt(level + EPSILON) * gain).astype(jnp.bfloat16)

def reference(queries, keys, values, q_gain, k_gain, frames, flags):
    q_norm = rms_rows(queries, q_gain).reshape(SPANS, T_C, HEADS, HD)
    k_norm = rms_rows(keys, k_gain).reshape(SPANS, T_C, HEADS, HD)
    value_all = values.reshape(SPANS, T_C, HEADS, HD)
    counts = frames.astype(jnp.int32) * FT
    sink_keys = k_norm[0, :FT]
    sink_values = value_all[0, :FT]
    slot_index = jnp.arange(T_C, dtype=jnp.int32)
    scaling = 1.0 / math.sqrt(HD)

    def one_span(span_index):
        before = jnp.maximum(span_index - 1, 0).astype(jnp.int32)
        earlier = jnp.maximum(span_index - 2, 0).astype(jnp.int32)
        n_current = counts[span_index]
        n_before = jnp.where(span_index >= 1, counts[before], 0).astype(jnp.int32)
        n_earlier = jnp.where(span_index >= 2, counts[earlier], 0).astype(jnp.int32)
        use_sink = flags[span_index, 0] > 0
        use_window = flags[span_index, 1] > 0
        key_set = jnp.concatenate([sink_keys, k_norm[earlier], k_norm[before], k_norm[span_index]], 0)
        value_set = jnp.concatenate([sink_values, value_all[earlier], value_all[before], value_all[span_index]], 0)
        allowed = jnp.concatenate([jnp.full((FT,), use_sink), use_window & (slot_index < n_earlier) & (slot_index >= n_before + n_earlier - WIN), use_window & (slot_index < n_before) & (slot_index >= n_before - WIN), slot_index < n_current])
        query_rows = q_norm[span_index].astype(jnp.float32)
        score = jnp.einsum('qhd,khd->hqk', query_rows, key_set.astype(jnp.float32)) * scaling
        score = jnp.where(allowed[None, None, :], score, -jnp.inf)
        highest = lax.optimization_barrier(jnp.max(score, axis=2, keepdims=True))
        weight = jnp.exp(score - highest).astype(jnp.bfloat16)
        denominator = lax.optimization_barrier(jnp.sum(weight.astype(jnp.float32), axis=2))
        blended = jnp.einsum('hqk,khd->qhd', weight.astype(jnp.float32), value_set.astype(jnp.float32))
        blended = blended / jnp.transpose(denominator)[:, :, None]
        blended = jnp.where((slot_index < n_current)[:, None, None], blended, 0.0)
        return blended.astype(jnp.bfloat16)
    span_blocks = lax.map(one_span, jnp.arange(SPANS, dtype=jnp.int32))
    return span_blocks.reshape(TOKENS, COLS)
```

```python
import math

import jax
import jax.numpy as jnp
from jax import lax
from jax.experimental import pallas as pl
from jax.experimental.pallas import tpu as pltpu
from jax.sharding import PartitionSpec as P

HD = 128
FT = 32
EPSILON = 1e-06
LANES = 128
VMEM = pl.BlockSpec(memory_space=pltpu.VMEM)
SMEM = pl.BlockSpec(memory_space=pltpu.SMEM)
PARAMS = pltpu.CompilerParams(vmem_limit_bytes=8 << 20)


def tree_rounds(count):
    top = 1
    while top * 2 < count:
        top *= 2
    strides = [1] if count > 1 else []
    while top >= 2:
        strides.append(top)
        top //= 2
    held, rounds = [0], []
    for stride in strides:
        pairs = [(h, h + stride) for h in held if h + stride < count and h + stride not in held]
        rounds.append((stride, pairs))
        held = held + [target for _, target in pairs]
    return rounds


def sums_kernel(q_ref, k_ref, sums_ref):
    rows = q_ref.shape[0]
    q = q_ref[...].astype(jnp.float32)
    k = k_ref[...].astype(jnp.float32)
    q_sum = jnp.sum(q * q, axis=1, keepdims=True)
    k_sum = jnp.sum(k * k, axis=1, keepdims=True)
    lane = lax.broadcasted_iota(jnp.int32, (rows, LANES), 1)
    sums_ref[...] = jnp.where(lane < LANES // 2, q_sum, k_sum)


def pack_kernel(full_width, frames_ref, q_ref, k_ref, v_ref, qg_ref, kg_ref, mine_ref, other_ref,
                qn_ref, kn_ref, sink_ref, near_ref, far_ref):
    cols = q_ref.shape[1]
    sums = mine_ref[...] + other_ref[...]
    factor = lax.rsqrt(sums / full_width + EPSILON)
    qn_ref[...] = (q_ref[...].astype(jnp.float32) * factor[:, :1] * qg_ref[...]).astype(jnp.bfloat16)
    kn = (k_ref[...].astype(jnp.float32) * factor[:, LANES // 2:LANES // 2 + 1] * kg_ref[...]).astype(jnp.bfloat16)
    kn_ref[...] = kn
    sink_ref[:, :cols] = kn[:FT]
    sink_ref[:, cols:] = v_ref[:FT, :]
    count = frames_ref[0]
    last = pl.multiple_of((count - 1) * FT, FT)
    before = pl.multiple_of(jnp.maximum(count - 2, 0) * FT, FT)
    mark = jnp.full((FT, LANES), count.astype(jnp.float32), jnp.float32).astype(jnp.bfloat16)
    last_k = kn_ref[pl.ds(last, FT), :]
    last_v = v_ref[pl.ds(last, FT), :]
    near_ref[:FT, :cols] = last_k
    near_ref[:FT, cols:2 * cols] = last_v
    near_ref[FT:, :cols] = kn_ref[pl.ds(before, FT), :]
    near_ref[FT:, cols:2 * cols] = v_ref[pl.ds(before, FT), :]
    near_ref[:FT, 2 * cols:] = mark
    near_ref[FT:, 2 * cols:] = mark
    far_ref[:, :cols] = last_k
    far_ref[:, cols:2 * cols] = last_v
    far_ref[:, 2 * cols:] = mark


def attend_kernel(frames_ref, flags_ref, q_ref, k_ref, v_ref, sink_ref, near_ref, far_ref, out_ref):
    rows, cols = q_ref.shape
    count = frames_ref[0]
    use_sink = flags_ref[0, 0] > 0
    use_window = flags_ref[0, 1] > 0
    span = rows + 3 * FT
    slot = lax.broadcasted_iota(jnp.int32, (1, span), 1)
    near_mark = jnp.max(near_ref[:1, 2 * cols:].astype(jnp.float32), axis=1, keepdims=True)
    far_mark = jnp.max(far_ref[:1, 2 * cols:].astype(jnp.float32), axis=1, keepdims=True)
    near_two = near_mark > 1.5
    window = jnp.where(use_window, 1.0, 0.0)
    sink = jnp.where(use_sink, 1.0, 0.0)
    has_last = near_mark * window
    has_before = jnp.where(near_two, near_mark, far_mark) * window
    allow = jnp.where(slot < count * FT, 1.0, 0.0)
    allow = jnp.where(slot >= rows, has_last, allow)
    allow = jnp.where(slot >= rows + FT, has_before, allow)
    allow = jnp.where(slot >= rows + 2 * FT, sink, allow)
    allowed = allow > 0.5
    live = lax.broadcasted_iota(jnp.int32, (rows, HD), 0) < count * FT
    pick = jnp.broadcast_to(near_mark, (FT, HD)) > 1.5
    scaling = 1.0 / math.sqrt(HD)
    for head in range(cols // HD):
        a, b = head * HD, (head + 1) * HD
        keys = jnp.concatenate(
            [k_ref[:, a:b], near_ref[:FT, a:b], jnp.where(pick, near_ref[FT:, a:b], far_ref[:, a:b]), sink_ref[:, a:b]], 0
        )
        a, b = cols + a, cols + b
        vals = jnp.concatenate(
            [v_ref[:, a - cols:b - cols], near_ref[:FT, a:b], jnp.where(pick, near_ref[FT:, a:b], far_ref[:, a:b]),
             sink_ref[:, a:b]], 0
        )
        score = lax.dot_general(
            q_ref[:, a - cols:b - cols], keys, (((1,), (1,)), ((), ())), preferred_element_type=jnp.float32
        ) * scaling
        score = jnp.where(allowed, score, -jnp.inf)
        weight = jnp.exp(score - jnp.max(score, axis=1, keepdims=True)).astype(jnp.bfloat16)
        denominator = jnp.sum(weight.astype(jnp.float32), axis=1, keepdims=True)
        blended = lax.dot_general(weight, vals, (((1,), (0,)), ((), ())), preferred_element_type=jnp.float32)
        out_ref[:, a - cols:b - cols] = jnp.where(live, blended / denominator, 0.0).astype(jnp.bfloat16)


def local(queries, keys, values, q_gain, k_gain, frames, flags):
    rows, cols = queries.shape
    full_width = cols * lax.axis_size("head")
    count = lax.axis_size("tm")
    heads = lax.axis_size("head")
    here = lax.axis_index("tm")
    f32, bf16 = jnp.float32, jnp.bfloat16
    shape = jax.ShapeDtypeStruct

    mine = pl.pallas_call(
        sums_kernel, out_shape=shape((rows, LANES), f32), in_specs=[VMEM] * 2, out_specs=VMEM, name="sums", compiler_params=PARAMS
    )(queries, keys)
    other = lax.ppermute(mine, "head", [(0, 1), (1, 0)])
    qn, kn, sink, near, far = pl.pallas_call(
        lambda *refs: pack_kernel(full_width, *refs),
        out_shape=(
            shape((rows, cols), bf16), shape((rows, cols), bf16), shape((FT, 2 * cols), bf16),
            shape((2 * FT, 2 * cols + LANES), bf16), shape((FT, 2 * cols + LANES), bf16),
        ),
        in_specs=[SMEM] + [VMEM] * 7, out_specs=(VMEM,) * 5, name="pack", compiler_params=PARAMS,
    )(frames, queries, keys, values, q_gain.reshape(1, cols), k_gain.reshape(1, cols), mine, other)

    near_in = lax.ppermute(near, "tm", [(i, i + 1) for i in range(count - 1)])
    far_in = lax.ppermute(far, "tm", [(i, i + 2) for i in range(count - 2)])
    held = here == 0
    for stride, pairs in tree_rounds(count):
        came = lax.ppermute(sink, "tm", pairs)
        sink = jnp.where(held, sink, came)
        held = here < 2 if stride == 1 else here % stride < 2
    return pl.pallas_call(
        attend_kernel, out_shape=shape((rows, cols), bf16), in_specs=[SMEM] * 2 + [VMEM] * 6, out_specs=VMEM, name="attend", compiler_params=PARAMS
    )(frames, flags, qn, kn, values, sink, near_in, far_in)


def solution(mesh):
    placed = (
        P(("groups", "tm"), "head"),
        P(("groups", "tm"), "head"),
        P(("groups", "tm"), "head"),
        P("head"),
        P("head"),
        P(("groups", "tm")),
        P(("groups", "tm"), None),
    )
    return jax.shard_map(
        local, mesh=mesh, in_specs=placed, out_specs=P(("groups", "tm"), "head"), check_vma=False
    )
```

```python
import math

import jax
import jax.numpy as jnp
from jax import lax
from jax.experimental import pallas as pl
from jax.experimental.pallas import tpu as pltpu
from jax.sharding import PartitionSpec as P


HD = 128
FT = 32
EPSILON = 1e-06
LANES = 128
VMEM = pl.BlockSpec(memory_space=pltpu.VMEM)
HBM = pl.BlockSpec(memory_space=pltpu.HBM)
PARAMS = pltpu.CompilerParams(vmem_limit_bytes=8 << 20)
F32 = jnp.float32
BF16 = jnp.bfloat16


def tree_rounds(count):
    top = 1
    while top * 2 < count:
        top *= 2
    strides = [1] if count > 1 else []
    while top >= 2:
        strides.append(top)
        top //= 2
    held, rounds = [0], []
    for stride in strides:
        pairs = [(h, h + stride) for h in held if h + stride < count and h + stride not in held]
        rounds.append((stride, pairs))
        held = held + [target for _, target in pairs]
    return rounds


def call(kernel, shapes, operands, specs=None, scratch=(), aliases=None):
    single = not isinstance(shapes, tuple)
    return pl.pallas_call(
        kernel,
        out_shape=shapes,
        in_specs=[VMEM] * len(operands) if specs is None else specs,
        out_specs=VMEM if single else (VMEM,) * len(shapes),
        scratch_shapes=list(scratch),
        input_output_aliases=aliases or {},
        compiler_params=PARAMS,
    )(*operands)


def lead_kernel(k_ref, v_ref, sink_ref, sums_ref, sem):
    cols = k_ref.shape[1]

    @pl.when(lax.axis_index("tm") == 0)
    def _():
        first = pltpu.make_async_copy(k_ref.at[:FT, :], sink_ref.at[:, :cols], sem.at[0])
        second = pltpu.make_async_copy(v_ref.at[:FT, :], sink_ref.at[:, cols:], sem.at[1])
        first.start()
        second.start()
        first.wait()
        k = sink_ref[:, :cols].astype(F32)
        sums_ref[...] = jnp.broadcast_to(jnp.sum(k * k, axis=1, keepdims=True), sums_ref.shape)
        second.wait()


def lead_norm_kernel(full_width, raw_ref, kg_ref, mine_ref, other_ref, sink_ref):
    cols = kg_ref.shape[1]

    @pl.when(lax.axis_index("tm") == 0)
    def _():
        factor = lax.rsqrt((mine_ref[:, :1] + other_ref[:, :1]) / full_width + EPSILON)
        sink_ref[:, :cols] = (raw_ref[:, :cols].astype(F32) * factor * kg_ref[...]).astype(BF16)
        sink_ref[:, cols:] = raw_ref[:, cols:]


def sums_kernel(q_ref, k_ref, sums_ref):
    q = q_ref[...].astype(F32)
    k = k_ref[...].astype(F32)
    q_sum = jnp.sum(q * q, axis=1, keepdims=True)
    k_sum = jnp.sum(k * k, axis=1, keepdims=True)
    lane = lax.broadcasted_iota(jnp.int32, sums_ref.shape, 1)
    sums_ref[...] = jnp.where(lane < LANES // 2, q_sum, k_sum)


def pack_kernel(full_width, frames_ref, q_ref, k_ref, v_ref, qg_ref, kg_ref, mine_ref, other_ref,
                qn_ref, kn_ref, near_ref, far_ref):
    rows, cols = q_ref.shape
    factor = lax.rsqrt((mine_ref[...] + other_ref[...]) / full_width + EPSILON)
    qn_ref[...] = (q_ref[...].astype(F32) * factor[:, :1] * qg_ref[...]).astype(BF16)
    kn_ref[...] = (k_ref[...].astype(F32) * factor[:, LANES // 2:LANES // 2 + 1] * kg_ref[...]).astype(BF16)
    count = frames_ref[...].reshape(1, 1).astype(F32)
    counts = jnp.broadcast_to(count, (FT, cols))
    mark = jnp.broadcast_to(count, (FT, LANES)).astype(BF16)
    for ref, at in ((kn_ref, 0), (v_ref, cols)):
        last, before = ref[:FT, :], ref[:FT, :]
        for frame in range(1, rows // FT):
            here = ref[frame * FT:(frame + 1) * FT, :]
            last = jnp.where(counts > frame + 0.5, here, last)
            before = jnp.where(counts > frame + 1.5, here, before)
        near_ref[:FT, at:at + cols] = last
        near_ref[FT:, at:at + cols] = before
        far_ref[:, at:at + cols] = last
    near_ref[:FT, 2 * cols:] = mark
    near_ref[FT:, 2 * cols:] = mark
    far_ref[:, 2 * cols:] = mark


def fold_kernel(frames_ref, flags_ref, q_ref, k_ref, v_ref, near_ref, far_ref, acc_ref, top_ref, den_ref):
    rows, cols = q_ref.shape
    span = rows + 2 * FT
    slot = lax.broadcasted_iota(jnp.int32, (1, span), 1)
    count = frames_ref[...].reshape(1, 1)
    window = jnp.where(flags_ref[:, 1:2] > 0, 1.0, 0.0)
    near_mark = near_ref[:1, 2 * cols:2 * cols + 1].astype(F32)
    far_mark = far_ref[:1, 2 * cols:2 * cols + 1].astype(F32)
    has_last = near_mark * window
    has_before = jnp.where(near_mark > 1.5, near_mark, far_mark) * window
    allow = jnp.where(slot < count * FT, 1.0, 0.0)
    allow = jnp.where(slot >= rows, has_last, allow)
    allow = jnp.where(slot >= rows + FT, has_before, allow)
    allowed = allow > 0.5
    pick = jnp.broadcast_to(near_mark, (FT, HD)) > 1.5
    ones = jnp.ones((span, HD), BF16)
    for head in range(cols // HD):
        a = head * HD
        b = a + HD
        near_k, far_k = near_ref[FT:, a:b], far_ref[:, a:b]
        keys = jnp.concatenate([k_ref[:, a:b], near_ref[:FT, a:b], jnp.where(pick, near_k, far_k)], 0)
        near_v, far_v = near_ref[FT:, cols + a:cols + b], far_ref[:, cols + a:cols + b]
        vals = jnp.concatenate([v_ref[:, a:b], near_ref[:FT, cols + a:cols + b], jnp.where(pick, near_v, far_v)], 0)
        score = lax.dot_general(
            q_ref[:, a:b], keys, (((1,), (1,)), ((), ())), preferred_element_type=F32
        ) * (1.0 / math.sqrt(HD))
        score = jnp.where(allowed, score, -jnp.inf)
        top = jnp.max(score, axis=1, keepdims=True)
        weight = jnp.exp(score - top).astype(BF16)
        both = jnp.dot(weight, jnp.concatenate([vals, ones], 1), preferred_element_type=F32)
        acc_ref[:, a:b] = both[:, :HD]
        den_ref[:, a:b] = both[:, HD:]
        top_ref[:, a:b] = jnp.broadcast_to(top, (rows, HD))


def finish_kernel(frames_ref, flags_ref, q_ref, sink_ref, acc_ref, top_ref, den_ref, out_ref):
    rows, cols = q_ref.shape
    use_sink = jnp.broadcast_to(flags_ref[:, 0:1], (rows, FT)) > 0
    live = lax.broadcasted_iota(jnp.int32, (rows, HD), 0) < frames_ref[...].reshape(1, 1) * FT
    ones = jnp.ones((FT, HD), BF16)
    for head in range(cols // HD):
        a = head * HD
        b = a + HD
        score = lax.dot_general(
            q_ref[:, a:b], sink_ref[:, a:b], (((1,), (1,)), ((), ())), preferred_element_type=F32
        ) * (1.0 / math.sqrt(HD))
        score = jnp.where(use_sink, score, -jnp.inf)
        old = top_ref[:, a:b]
        top = jnp.maximum(old, jnp.max(score, axis=1, keepdims=True))
        weight = jnp.exp(score - top[:, :FT]).astype(BF16)
        both = jnp.dot(
            weight, jnp.concatenate([sink_ref[:, cols + a:cols + b], ones], 1), preferred_element_type=F32
        )
        keep = jnp.exp(old - top)
        blended = (acc_ref[:, a:b] * keep + both[:, :HD]) / (den_ref[:, a:b] * keep + both[:, HD:])
        out_ref[:, a:b] = jnp.where(live, blended, 0.0).astype(BF16)


def local(queries, keys, values, q_gain, k_gain, frames, flags):
    rows, cols = queries.shape
    heads = lax.axis_size("head")
    full_width = cols * heads
    count = lax.axis_size("tm")
    here = lax.axis_index("tm")
    shape = jax.ShapeDtypeStruct
    q_gain, k_gain = q_gain.reshape(1, cols), k_gain.reshape(1, cols)
    swap = [(h, (h + 1) % heads) for h in range(heads)]

    raw, mine = call(
        lead_kernel, (shape((FT, 2 * cols), BF16), shape((FT, LANES), F32)),
        (pltpu.with_memory_space_constraint(keys, pltpu.HBM), pltpu.with_memory_space_constraint(values, pltpu.HBM)),
        specs=[HBM, HBM], scratch=[pltpu.SemaphoreType.DMA((2,))],
    )
    other = lax.ppermute(mine, ("tm", "head"), swap)
    sink = call(
        lambda *refs: lead_norm_kernel(full_width, *refs), shape((FT, 2 * cols), BF16),
        (raw, k_gain, mine, other),
    )
    mine = call(sums_kernel, shape((rows, LANES), F32), (queries, keys))
    other = lax.ppermute(mine, "head", swap)
    qn, kn, near, far = call(
        lambda *refs: pack_kernel(full_width, *refs),
        (
            shape((rows, cols), BF16), shape((rows, cols), BF16),
            shape((2 * FT, 2 * cols + LANES), BF16), shape((FT, 2 * cols + LANES), BF16),
        ),
        (frames, queries, keys, values, q_gain, k_gain, mine, other),
    )
    near = lax.ppermute(near, "tm", [(i, i + 1) for i in range(count - 1)])
    far = lax.ppermute(far, "tm", [(i, i + 2) for i in range(count - 2)])
    rounds = tree_rounds(count)
    held = here == 0
    for stride, pairs in rounds:
        came = lax.ppermute(sink, "tm", pairs)
        sink = jnp.where(held, sink, came)
        held = here < 2 if stride == 1 else here % stride < 2
    acc, top, den = call(fold_kernel, (shape((rows, cols), F32),) * 3, (frames, flags, qn, kn, values, near, far))
    return call(finish_kernel, shape((rows, cols), BF16), (frames, flags, qn, sink, acc, top, den))


def solution(mesh):
    placed = (
        P(("groups", "tm"), "head"),
        P(("groups", "tm"), "head"),
        P(("groups", "tm"), "head"),
        P("head"),
        P("head"),
        P(("groups", "tm")),
        P(("groups", "tm"), None),
    )
    return jax.shard_map(
        local, mesh=mesh, in_specs=placed, out_specs=P(("groups", "tm"), "head"), check_vma=False
    )
```

```python
import math

import jax
import jax.numpy as jnp
from jax import lax
from jax.experimental import pallas as pl
from jax.experimental.pallas import tpu as pltpu
from jax.sharding import PartitionSpec as P


HD = 128
FT = 32
EPSILON = 1e-06
LANES = 128
VMEM = pl.BlockSpec(memory_space=pltpu.VMEM)
HBM = pl.BlockSpec(memory_space=pltpu.HBM)
SMEM = pl.BlockSpec(memory_space=pltpu.SMEM)
PARAMS = pltpu.CompilerParams(vmem_limit_bytes=8 << 20)
F32 = jnp.float32
BF16 = jnp.bfloat16


def tree_rounds(count):
    top = 1
    while top * 2 < count:
        top *= 2
    strides = [2] if count > 2 else []
    while top >= 4:
        strides.append(top)
        top //= 2
    strides.append(1)
    held, rounds = [0], []
    for number, stride in enumerate(strides):
        pairs = [(h, h + stride) for h in held if h + stride < count and h + stride not in held]
        period, width = (count, 1) if number == 0 else (2, 1) if stride == 1 else (2 * stride, 4)
        rounds.append((pairs, period, width))
        held = sorted(held + [target for _, target in pairs])
    return rounds


def call(kernel, shapes, operands, specs=None, scratch=(), out_specs=None):
    single = not isinstance(shapes, tuple)
    return pl.pallas_call(
        kernel,
        out_shape=shapes,
        in_specs=[VMEM] * len(operands) if specs is None else specs,
        out_specs=out_specs or (VMEM if single else (VMEM,) * len(shapes)),
        scratch_shapes=list(scratch),
        compiler_params=PARAMS,
    )(*operands)


def load_kernel(q_hbm, k_hbm, v_hbm, flags_hbm, q_ref, k_ref, v_ref, sums_ref, ctl_ref, flags_ref, sem):
    copies = [
        pltpu.make_async_copy(source, target, sem.at[i])
        for i, (source, target) in enumerate(
            ((q_hbm, q_ref), (k_hbm, k_ref), (v_hbm, v_ref), (flags_hbm, flags_ref))
        )
    ]
    for copy in copies:
        copy.start()
    lane = lax.broadcasted_iota(jnp.int32, sums_ref.shape, 1)
    copies[0].wait()
    q = q_ref[...].astype(F32)
    q_sum = jnp.sum(q * q, axis=1, keepdims=True)
    copies[1].wait()
    k = k_ref[...].astype(F32)
    k_sum = jnp.sum(k * k, axis=1, keepdims=True)
    sums_ref[...] = jnp.where(lane < LANES // 2, q_sum, k_sum)
    copies[3].wait()
    row = lax.broadcasted_iota(jnp.int32, ctl_ref.shape, 0)
    ctl_ref[...] = jnp.where(row == 1, flags_ref[0, 0], flags_ref[0, 1]).astype(F32)
    copies[2].wait()


def pack_kernel(full_width, frames_ref, flags_ref, q_ref, k_ref, v_ref, qg_ref, kg_ref, mine_ref, other_ref,
                ctl_ref, qn_ref, kn_ref, sink_k_ref, sink_v_ref, near_ref, far_ref):
    rows, cols = q_ref.shape
    factor = lax.rsqrt((mine_ref[...] + other_ref[...]) / full_width + EPSILON)
    qn_ref[...] = (q_ref[...].astype(F32) * factor[:, :1] * qg_ref[...]).astype(BF16)
    kn_ref[...] = (k_ref[...].astype(F32) * factor[:, LANES // 2:LANES // 2 + 1] * kg_ref[...]).astype(BF16)
    sink_k_ref[...] = kn_ref[:FT, :]
    sink_v_ref[...] = v_ref[:FT, :]
    row = lax.broadcasted_iota(jnp.int32, ctl_ref.shape, 0)
    ctl = jnp.where(row == 0, frames_ref[0].astype(F32), flags_ref[...])
    ctl_ref[...] = ctl
    count = ctl[:1, :1]
    counts = jnp.broadcast_to(count, (FT, cols))
    mark = jnp.broadcast_to(count, (FT, LANES)).astype(BF16)
    for ref, at in ((kn_ref, 0), (v_ref, cols)):
        last, before = ref[:FT, :], ref[:FT, :]
        for frame in range(1, rows // FT):
            here = ref[frame * FT:(frame + 1) * FT, :]
            last = jnp.where(counts > frame + 0.5, here, last)
            before = jnp.where(counts > frame + 1.5, here, before)
        near_ref[:FT, at:at + cols] = last
        near_ref[FT:, at:at + cols] = before
        far_ref[:, at:at + cols] = last
    near_ref[:FT, 2 * cols:] = mark
    near_ref[FT:, 2 * cols:] = mark
    far_ref[:, 2 * cols:] = mark


def own_kernel(ctl_ref, q_ref, k_ref, v_ref, acc_ref, top_ref, den_ref):
    rows, cols = q_ref.shape
    slot = lax.broadcasted_iota(jnp.int32, (rows, rows), 1).astype(F32)
    allowed = slot < ctl_ref[:1, :1] * FT
    ones = jnp.ones((rows, HD), BF16)
    for a in range(0, cols, HD):
        b = a + HD
        score = lax.dot_general(
            q_ref[:, a:b], k_ref[:, a:b], (((1,), (1,)), ((), ())), preferred_element_type=F32
        ) * (1.0 / math.sqrt(HD))
        score = jnp.where(allowed, score, -jnp.inf)
        top = jnp.max(score, axis=1, keepdims=True)
        weight = jnp.exp(score - top).astype(BF16)
        both = jnp.dot(weight, jnp.concatenate([v_ref[:, a:b], ones], 1), preferred_element_type=F32)
        acc_ref[:, a:b] = both[:, :HD]
        den_ref[:, a:b] = both[:, HD:]
        top_ref[:, a:b] = jnp.broadcast_to(top, (rows, HD))


def finish_kernel(ctl_ref, q_ref, sink_k_ref, sink_v_ref, near_ref, far_ref, acc_ref, top_ref, den_ref, out_ref):
    rows, cols = q_ref.shape
    span = 3 * FT
    count = ctl_ref[:1, :1]
    sink = ctl_ref[1:2, :1]
    window = ctl_ref[2:3, :1]
    near_mark = near_ref[:1, 2 * cols:2 * cols + 1].astype(F32)
    far_mark = far_ref[:1, 2 * cols:2 * cols + 1].astype(F32)
    has_before = jnp.where(near_mark > 1.5, near_mark, far_mark) * window
    slot = lax.broadcasted_iota(jnp.int32, (rows, span), 1)
    allow = jnp.where(slot < FT, near_mark * window, jnp.where(slot < 2 * FT, has_before, sink))
    allowed = allow > 0.5
    live = lax.broadcasted_iota(jnp.int32, (rows, HD), 0).astype(F32) < count * FT
    pick = jnp.broadcast_to(near_mark, (FT, HD)) > 1.5
    ones = jnp.ones((span, HD), BF16)
    for a in range(0, cols, HD):
        b = a + HD
        before = jnp.where(pick, near_ref[FT:, a:b], far_ref[:, a:b])
        keys = jnp.concatenate([near_ref[:FT, a:b], before, sink_k_ref[:, a:b]], 0)
        before = jnp.where(pick, near_ref[FT:, cols + a:cols + b], far_ref[:, cols + a:cols + b])
        vals = jnp.concatenate([near_ref[:FT, cols + a:cols + b], before, sink_v_ref[:, a:b]], 0)
        score = lax.dot_general(
            q_ref[:, a:b], keys, (((1,), (1,)), ((), ())), preferred_element_type=F32
        ) * (1.0 / math.sqrt(HD))
        score = jnp.where(allowed, score, -jnp.inf)
        old = top_ref[:, a:b]
        top = jnp.maximum(old, jnp.max(score, axis=1, keepdims=True))
        weight = jnp.exp(score - top[:, :span]).astype(BF16)
        both = jnp.dot(weight, jnp.concatenate([vals, ones], 1), preferred_element_type=F32)
        keep = jnp.exp(old - top)
        blended = (acc_ref[:, a:b] * keep + both[:, :HD]) / (den_ref[:, a:b] * keep + both[:, HD:])
        out_ref[:, a:b] = jnp.where(live, blended, 0.0).astype(BF16)


def local(queries, keys, values, q_gain, k_gain, frames, flags):
    rows, cols = queries.shape
    heads = lax.axis_size("head")
    full_width = cols * heads
    count = lax.axis_size("tm")
    here = lax.axis_index("tm")
    shape = jax.ShapeDtypeStruct
    block = shape((rows, cols), BF16)
    wide = shape((rows, cols), F32)
    q_gain, k_gain = q_gain.reshape(1, cols), k_gain.reshape(1, cols)
    in_hbm = lambda x: pltpu.with_memory_space_constraint(x, pltpu.HBM)

    q, k, v, mine, ctl_flags = call(
        load_kernel, (block, block, block, shape((rows, LANES), F32), shape((8, LANES), F32)),
        tuple(in_hbm(x) for x in (queries, keys, values, flags)), specs=[HBM] * 4,
        scratch=[pltpu.SMEM((1, 2), jnp.int32), pltpu.SemaphoreType.DMA((4,))],
    )
    other = lax.ppermute(mine, "head", [(h, (h + 1) % heads) for h in range(heads)])
    ctl, qn, kn, sink_k, sink_v, near, far = call(
        lambda *refs: pack_kernel(full_width, *refs),
        (
            shape((8, LANES), F32), block, block, shape((FT, cols), BF16), shape((FT, cols), BF16),
            shape((2 * FT, 2 * cols + LANES), BF16), shape((FT, 2 * cols + LANES), BF16),
        ),
        (frames, ctl_flags, q, k, v, q_gain, k_gain, mine, other), specs=[SMEM] + [VMEM] * 8,
    )
    near = lax.ppermute(near, "tm", [(i, i + 1) for i in range(count - 1)])
    far = lax.ppermute(far, "tm", [(i, i + 2) for i in range(count - 2)])
    rounds = tree_rounds(count)
    for pairs, period, width in rounds:
        came_k = lax.ppermute(sink_k, "tm", pairs)
        came_v = lax.ppermute(sink_v, "tm", pairs)
        kept = here % period < width
        sink_k = jnp.where(kept, sink_k, came_k)
        sink_v = jnp.where(kept, sink_v, came_v)
    acc, top, den = call(own_kernel, (wide, wide, wide), (ctl, qn, kn, v))
    return call(finish_kernel, block, (ctl, qn, sink_k, sink_v, near, far, acc, top, den))


def solution(mesh):
    placed = (
        P(("groups", "tm"), "head"),
        P(("groups", "tm"), "head"),
        P(("groups", "tm"), "head"),
        P("head"),
        P("head"),
        P(("groups", "tm")),
        P(("groups", "tm"), None),
    )
    return jax.shard_map(
        local, mesh=mesh, in_specs=placed, out_specs=P(("groups", "tm"), "head"), check_vma=False
    )
```

```python
import math

import jax
import jax.numpy as jnp
from jax import lax
from jax.experimental import pallas as pl
from jax.experimental.pallas import tpu as pltpu
from jax.sharding import PartitionSpec as P


HD = 128
FT = 32
EPSILON = 1e-06
LANES = 128
VMEM = pl.BlockSpec(memory_space=pltpu.VMEM)
HBM = pl.BlockSpec(memory_space=pltpu.HBM)
SMEM = pl.BlockSpec(memory_space=pltpu.SMEM)
PARAMS = pltpu.CompilerParams(vmem_limit_bytes=8 << 20)
F32 = jnp.float32
BF16 = jnp.bfloat16


def tree_rounds(count):
    stride = 1
    while stride * 2 < count:
        stride *= 2
    held, rounds = [0], []
    while stride:
        pairs = [(h, h + stride) for h in held if h + stride < count]
        rounds.append((pairs, 2 * stride))
        held = sorted(held + [target for _, target in pairs])
        stride //= 2
    return rounds


def call(kernel, shapes, operands, specs=None, scratch=(), out_specs=None):
    single = not isinstance(shapes, tuple)
    return pl.pallas_call(
        kernel,
        out_shape=shapes,
        in_specs=[VMEM] * len(operands) if specs is None else specs,
        out_specs=out_specs or (VMEM if single else (VMEM,) * len(shapes)),
        scratch_shapes=list(scratch),
        compiler_params=PARAMS,
    )(*operands)


def load_kernel(q_hbm, k_hbm, v_hbm, flags_hbm, q_ref, k_ref, v_ref, sums_ref, ctl_ref, flags_ref, sem):
    copies = [
        pltpu.make_async_copy(source, target, sem.at[i])
        for i, (source, target) in enumerate(
            ((q_hbm, q_ref), (k_hbm, k_ref), (v_hbm, v_ref), (flags_hbm, flags_ref))
        )
    ]
    for copy in copies:
        copy.start()
    lane = lax.broadcasted_iota(jnp.int32, sums_ref.shape, 1)
    copies[0].wait()
    q = q_ref[...].astype(F32)
    q_sum = jnp.sum(q * q, axis=1, keepdims=True)
    copies[1].wait()
    k = k_ref[...].astype(F32)
    k_sum = jnp.sum(k * k, axis=1, keepdims=True)
    sums_ref[...] = jnp.where(lane < LANES // 2, q_sum, k_sum)
    copies[3].wait()
    row = lax.broadcasted_iota(jnp.int32, ctl_ref.shape, 0)
    ctl_ref[...] = jnp.where(row == 1, flags_ref[0, 0], flags_ref[0, 1]).astype(F32)
    copies[2].wait()


def pack_kernel(full_width, frames_ref, flags_ref, q_ref, k_ref, v_ref, qg_ref, kg_ref, mine_ref, other_ref,
                ctl_ref, qn_ref, kn_ref, sink_k_ref, sink_v_ref, near_ref, far_ref):
    rows, cols = q_ref.shape
    factor = lax.rsqrt((mine_ref[...] + other_ref[...]) / full_width + EPSILON)
    qn_ref[...] = (q_ref[...].astype(F32) * factor[:, :1] * qg_ref[...]).astype(BF16)
    kn_ref[...] = (k_ref[...].astype(F32) * factor[:, LANES // 2:LANES // 2 + 1] * kg_ref[...]).astype(BF16)
    sink_k_ref[...] = kn_ref[:FT, :]
    sink_v_ref[...] = v_ref[:FT, :]
    row = lax.broadcasted_iota(jnp.int32, ctl_ref.shape, 0)
    ctl = jnp.where(row == 0, frames_ref[0].astype(F32), flags_ref[...])
    ctl_ref[...] = ctl
    count = ctl[:1, :1]
    counts = jnp.broadcast_to(count, (FT, cols))
    mark = jnp.broadcast_to(count, (FT, LANES)).astype(BF16)
    for ref, at in ((kn_ref, 0), (v_ref, cols)):
        last, before = ref[:FT, :], ref[:FT, :]
        for frame in range(1, rows // FT):
            here = ref[frame * FT:(frame + 1) * FT, :]
            last = jnp.where(counts > frame + 0.5, here, last)
            before = jnp.where(counts > frame + 1.5, here, before)
        near_ref[:FT, at:at + cols] = last
        near_ref[FT:, at:at + cols] = before
        far_ref[:, at:at + cols] = last
    near_ref[:FT, 2 * cols:] = mark
    near_ref[FT:, 2 * cols:] = mark
    far_ref[:, 2 * cols:] = mark


def own_kernel(ctl_ref, q_ref, k_ref, v_ref, acc_ref, top_ref, den_ref, score_ref, weight_ref):
    rows, cols = q_ref.shape
    heads = [(i, i * HD, (i + 1) * HD) for i in range(cols // HD)]
    slot = lax.broadcasted_iota(jnp.int32, (rows, rows), 1).astype(F32)
    allowed = slot < ctl_ref[:1, :1] * FT
    ones = jnp.ones((rows, HD), BF16)
    for i, a, b in heads:
        score = lax.dot_general(
            q_ref[:, a:b], k_ref[:, a:b], (((1,), (1,)), ((), ())), preferred_element_type=F32
        ) * (1.0 / math.sqrt(HD))
        score_ref[i] = jnp.where(allowed, score, -jnp.inf)
    for i, a, b in heads:
        score = score_ref[i]
        top = jnp.max(score, axis=1, keepdims=True)
        top_ref[:, a:b] = jnp.broadcast_to(top, (rows, HD))
        weight_ref[i] = jnp.exp(score - top).astype(BF16)
    for i, a, b in heads:
        both = jnp.dot(weight_ref[i], jnp.concatenate([v_ref[:, a:b], ones], 1), preferred_element_type=F32)
        acc_ref[:, a:b] = both[:, :HD]
        den_ref[:, a:b] = both[:, HD:]


def finish_kernel(ctl_ref, q_ref, sink_k_ref, sink_v_ref, near_ref, far_ref, acc_ref, top_ref, den_ref, out_ref,
                  score_ref, weight_ref, keep_ref):
    rows, cols = q_ref.shape
    span = 3 * FT
    heads = [(i, i * HD, (i + 1) * HD) for i in range(cols // HD)]
    count = ctl_ref[:1, :1]
    sink = ctl_ref[1:2, :1]
    window = ctl_ref[2:3, :1]
    near_mark = near_ref[:1, 2 * cols:2 * cols + 1].astype(F32)
    far_mark = far_ref[:1, 2 * cols:2 * cols + 1].astype(F32)
    has_before = jnp.where(near_mark > 1.5, near_mark, far_mark) * window
    slot = lax.broadcasted_iota(jnp.int32, (rows, span), 1)
    allow = jnp.where(slot < FT, near_mark * window, jnp.where(slot < 2 * FT, has_before, sink))
    allowed = allow > 0.5
    live = lax.broadcasted_iota(jnp.int32, (rows, HD), 0).astype(F32) < count * FT
    pick = jnp.broadcast_to(near_mark, (FT, HD)) > 1.5
    ones = jnp.ones((span, HD), BF16)
    for i, a, b in heads:
        before = jnp.where(pick, near_ref[FT:, a:b], far_ref[:, a:b])
        keys = jnp.concatenate([near_ref[:FT, a:b], before, sink_k_ref[:, a:b]], 0)
        score = lax.dot_general(
            q_ref[:, a:b], keys, (((1,), (1,)), ((), ())), preferred_element_type=F32
        ) * (1.0 / math.sqrt(HD))
        score_ref[i] = jnp.where(allowed, score, -jnp.inf)
    for i, a, b in heads:
        score = score_ref[i]
        old = top_ref[:, a:b]
        top = jnp.maximum(old, jnp.max(score, axis=1, keepdims=True))
        keep_ref[i] = jnp.exp(old - top)
        weight_ref[i] = jnp.exp(score - top[:, :span]).astype(BF16)
    for i, a, b in heads:
        before = jnp.where(pick, near_ref[FT:, cols + a:cols + b], far_ref[:, cols + a:cols + b])
        vals = jnp.concatenate([near_ref[:FT, cols + a:cols + b], before, sink_v_ref[:, a:b]], 0)
        both = jnp.dot(weight_ref[i], jnp.concatenate([vals, ones], 1), preferred_element_type=F32)
        keep = keep_ref[i]
        blended = (acc_ref[:, a:b] * keep + both[:, :HD]) / (den_ref[:, a:b] * keep + both[:, HD:])
        out_ref[:, a:b] = jnp.where(live, blended, 0.0).astype(BF16)


def local(queries, keys, values, q_gain, k_gain, frames, flags):
    rows, cols = queries.shape
    heads = lax.axis_size("head")
    full_width = cols * heads
    count = lax.axis_size("tm")
    here = lax.axis_index("tm")
    shape = jax.ShapeDtypeStruct
    block = shape((rows, cols), BF16)
    wide = shape((rows, cols), F32)
    q_gain, k_gain = q_gain.reshape(1, cols), k_gain.reshape(1, cols)
    in_hbm = lambda x: pltpu.with_memory_space_constraint(x, pltpu.HBM)

    q, k, v, mine, ctl_flags = call(
        load_kernel, (block, block, block, shape((rows, LANES), F32), shape((8, LANES), F32)),
        tuple(in_hbm(x) for x in (queries, keys, values, flags)), specs=[HBM] * 4,
        scratch=[pltpu.SMEM((1, 2), jnp.int32), pltpu.SemaphoreType.DMA((4,))],
    )
    other = lax.ppermute(mine, "head", [(h, (h + 1) % heads) for h in range(heads)])
    ctl, qn, kn, sink_k, sink_v, near, far = call(
        lambda *refs: pack_kernel(full_width, *refs),
        (
            shape((8, LANES), F32), block, block, shape((FT, cols), BF16), shape((FT, cols), BF16),
            shape((2 * FT, 2 * cols + LANES), BF16), shape((FT, 2 * cols + LANES), BF16),
        ),
        (frames, ctl_flags, q, k, v, q_gain, k_gain, mine, other), specs=[SMEM] + [VMEM] * 8,
    )
    near = lax.ppermute(near, "tm", [(i, i + 1) for i in range(count - 1)])
    far = lax.ppermute(far, "tm", [(i, i + 2) for i in range(count - 2)])
    rounds = tree_rounds(count)
    for pairs, period in rounds:
        came_k = lax.ppermute(sink_k, "tm", pairs)
        came_v = lax.ppermute(sink_v, "tm", pairs)
        kept = here % period == 0
        sink_k = jnp.where(kept, sink_k, came_k)
        sink_v = jnp.where(kept, sink_v, came_v)
    acc, top, den = call(
        own_kernel, (wide, wide, wide), (ctl, qn, kn, v),
        scratch=[pltpu.VMEM((cols // HD, rows, rows), F32), pltpu.VMEM((cols // HD, rows, rows), BF16)],
    )
    return call(
        finish_kernel, block, (ctl, qn, sink_k, sink_v, near, far, acc, top, den),
        scratch=[
            pltpu.VMEM((cols // HD, rows, 3 * FT), F32), pltpu.VMEM((cols // HD, rows, 3 * FT), BF16),
            pltpu.VMEM((cols // HD, rows, HD), F32),
        ],
    )


def solution(mesh):
    placed = (
        P(("groups", "tm"), "head"),
        P(("groups", "tm"), "head"),
        P(("groups", "tm"), "head"),
        P("head"),
        P("head"),
        P(("groups", "tm")),
        P(("groups", "tm"), None),
    )
    return jax.shard_map(
        local, mesh=mesh, in_specs=placed, out_specs=P(("groups", "tm"), "head"), check_vma=False
    )
```

```python
import math

import jax
import jax.numpy as jnp
from jax import lax
from jax.experimental import pallas as pl
from jax.experimental.pallas import tpu as pltpu
from jax.sharding import PartitionSpec as P


HD = 128
FT = 32
EPSILON = 1e-06
LANES = 128
VMEM = pl.BlockSpec(memory_space=pltpu.VMEM)
HBM = pl.BlockSpec(memory_space=pltpu.HBM)
SMEM = pl.BlockSpec(memory_space=pltpu.SMEM)
PARAMS = pltpu.CompilerParams(vmem_limit_bytes=8 << 20)
F32 = jnp.float32
BF16 = jnp.bfloat16


def tree_rounds(count):
    stride = 1
    while stride * 2 < count:
        stride *= 2
    held, rounds = [0], []
    while stride:
        pairs = [(h, h + stride) for h in held if h + stride < count]
        rounds.append((pairs, 2 * stride))
        held = sorted(held + [target for _, target in pairs])
        stride //= 2
    return rounds


def call(kernel, shapes, operands, specs=None, scratch=(), out_specs=None):
    single = not isinstance(shapes, tuple)
    return pl.pallas_call(
        kernel,
        out_shape=shapes,
        in_specs=[VMEM] * len(operands) if specs is None else specs,
        out_specs=out_specs or (VMEM if single else (VMEM,) * len(shapes)),
        scratch_shapes=list(scratch),
        compiler_params=PARAMS,
    )(*operands)


def lead_kernel(k_hbm, v_hbm, sink_k_ref, sink_v_ref, sink_ref, sem):
    cols = k_hbm.shape[1]

    @pl.when(lax.axis_index("tm") == 0)
    def _():
        first = pltpu.make_async_copy(k_hbm.at[:FT, :], sink_k_ref, sem.at[0])
        second = pltpu.make_async_copy(v_hbm.at[:FT, :], sink_v_ref, sem.at[1])
        first.start()
        second.start()
        first.wait()
        second.wait()
        sink_ref[:, :cols] = sink_k_ref[...]
        sink_ref[:, cols:] = sink_v_ref[...]


def pack_kernel(frames_ref, k_ref, v_ref, near_ref, far_ref):
    rows, cols = k_ref.shape
    count = jnp.full((1, 1), frames_ref[0].astype(F32))
    counts = jnp.broadcast_to(count, (FT, cols))
    mark = jnp.broadcast_to(count, (FT, LANES)).astype(BF16)
    for ref, at in ((k_ref, 0), (v_ref, cols)):
        last, before = ref[:FT, :], ref[:FT, :]
        for frame in range(1, rows // FT):
            here = ref[frame * FT:(frame + 1) * FT, :]
            last = jnp.where(counts > frame + 0.5, here, last)
            before = jnp.where(counts > frame + 1.5, here, before)
        near_ref[:FT, at:at + cols] = last
        near_ref[FT:, at:at + cols] = before
        far_ref[:, at:at + cols] = last
    near_ref[:FT, 2 * cols:] = mark
    near_ref[FT:, 2 * cols:] = mark
    far_ref[:, 2 * cols:] = mark


def square_sums(ref):
    x = ref[...].astype(F32)
    return jnp.sum(x * x, axis=1, keepdims=True)


def sums_kernel(q_ref, k_ref, sums_ref):
    lane = lax.broadcasted_iota(jnp.int32, sums_ref.shape, 1)
    sums_ref[...] = jnp.where(lane < LANES // 2, square_sums(q_ref), square_sums(k_ref))


def own_kernel(full_width, frames_ref, flags_ref, q_ref, k_ref, v_ref, qg_ref, kg_ref, mine_ref, other_ref,
               ctl_ref, qn_ref, acc_ref, top_ref, den_ref, kn_ref, score_ref, weight_ref):
    rows, cols = q_ref.shape
    flags = flags_ref[...].astype(F32)
    row = lax.broadcasted_iota(jnp.int32, ctl_ref.shape, 0)
    ctl_ref[...] = jnp.where(row == 0, flags[:, :1], flags[:, 1:2])
    factor = lax.rsqrt((mine_ref[...] + other_ref[...]) / full_width + EPSILON)
    qn_ref[...] = (q_ref[...].astype(F32) * factor[:, :1] * qg_ref[...]).astype(BF16)
    kn_ref[...] = (k_ref[...].astype(F32) * factor[:, LANES // 2:LANES // 2 + 1] * kg_ref[...]).astype(BF16)
    heads = [(i, i * HD, (i + 1) * HD) for i in range(cols // HD)]
    allowed = lax.broadcasted_iota(jnp.int32, (rows, rows), 1) < frames_ref[0] * FT
    ones = jnp.ones((rows, HD), BF16)
    for i, a, b in heads:
        score = lax.dot_general(
            qn_ref[:, a:b], kn_ref[:, a:b], (((1,), (1,)), ((), ())), preferred_element_type=F32
        ) * (1.0 / math.sqrt(HD))
        score_ref[i] = jnp.where(allowed, score, -jnp.inf)
    for i, a, b in heads:
        score = score_ref[i]
        top = jnp.max(score, axis=1, keepdims=True)
        top_ref[:, a:b] = jnp.broadcast_to(top, (rows, HD))
        weight_ref[i] = jnp.exp(score - top).astype(BF16)
    for i, a, b in heads:
        both = jnp.dot(weight_ref[i], jnp.concatenate([v_ref[:, a:b], ones], 1), preferred_element_type=F32)
        acc_ref[:, a:b] = both[:, :HD]
        den_ref[:, a:b] = both[:, HD:]


def gather_kernel(near_ref, far_ref, sink_k_ref, next_ref, keys_ref, sums_ref):
    cols = sink_k_ref.shape[1]
    pick = jnp.broadcast_to(near_ref[:1, 2 * cols:2 * cols + 1].astype(F32), (FT, cols)) > 1.5
    second = jnp.full((FT, cols), lax.axis_index("tm"), jnp.int32) == 1
    keys_ref[:FT, :] = near_ref[:FT, :cols]
    keys_ref[FT:2 * FT, :] = jnp.where(pick, near_ref[FT:, :cols], far_ref[:, :cols])
    keys_ref[2 * FT:, :] = jnp.where(second, next_ref[:, :cols], sink_k_ref[...])
    sums_ref[...] = jnp.broadcast_to(square_sums(keys_ref), sums_ref.shape)


def finish_kernel(full_width, frames_ref, ctl_ref, q_ref, raw_ref, kg_ref, mine_ref, other_ref, sink_v_ref, next_ref,
                  near_ref, far_ref, acc_ref, top_ref, den_ref, out_ref, keys_ref, score_ref, weight_ref, keep_ref):
    rows, cols = q_ref.shape
    span = 3 * FT
    factor = lax.rsqrt((mine_ref[:, :1] + other_ref[:, :1]) / full_width + EPSILON)
    keys_ref[...] = (raw_ref[...].astype(F32) * factor * kg_ref[...]).astype(BF16)
    heads = [(i, i * HD, (i + 1) * HD) for i in range(cols // HD)]
    sink = ctl_ref[:1, :1]
    window = ctl_ref[1:2, :1]
    near_mark = near_ref[:1, 2 * cols:2 * cols + 1].astype(F32)
    far_mark = far_ref[:1, 2 * cols:2 * cols + 1].astype(F32)
    has_before = jnp.where(near_mark > 1.5, near_mark, far_mark) * window
    slot = lax.broadcasted_iota(jnp.int32, (rows, span), 1)
    allow = jnp.where(slot < FT, near_mark * window, jnp.where(slot < 2 * FT, has_before, sink))
    allowed = allow > 0.5
    live = lax.broadcasted_iota(jnp.int32, (rows, HD), 0) < frames_ref[0] * FT
    pick = jnp.broadcast_to(near_mark, (FT, HD)) > 1.5
    second = jnp.full((FT, HD), lax.axis_index("tm"), jnp.int32) == 1
    ones = jnp.ones((span, HD), BF16)
    for i, a, b in heads:
        score = lax.dot_general(
            q_ref[:, a:b], keys_ref[:, a:b], (((1,), (1,)), ((), ())), preferred_element_type=F32
        ) * (1.0 / math.sqrt(HD))
        score_ref[i] = jnp.where(allowed, score, -jnp.inf)
    for i, a, b in heads:
        score = score_ref[i]
        old = top_ref[:, a:b]
        top = jnp.maximum(old, jnp.max(score, axis=1, keepdims=True))
        keep_ref[i] = jnp.exp(old - top)
        weight_ref[i] = jnp.exp(score - top[:, :span]).astype(BF16)
    for i, a, b in heads:
        c, d = cols + a, cols + b
        before = jnp.where(pick, near_ref[FT:, c:d], far_ref[:, c:d])
        first = jnp.where(second, next_ref[:, c:d], sink_v_ref[:, a:b])
        vals = jnp.concatenate([near_ref[:FT, c:d], before, first], 0)
        both = jnp.dot(weight_ref[i], jnp.concatenate([vals, ones], 1), preferred_element_type=F32)
        keep = keep_ref[i]
        blended = (acc_ref[:, a:b] * keep + both[:, :HD]) / (den_ref[:, a:b] * keep + both[:, HD:])
        out_ref[:, a:b] = jnp.where(live, blended, 0.0).astype(BF16)


def local(queries, keys, values, q_gain, k_gain, frames, flags):
    rows, cols = queries.shape
    heads = lax.axis_size("head")
    full_width = cols * heads
    count = lax.axis_size("tm")
    here = lax.axis_index("tm")
    shape = jax.ShapeDtypeStruct
    block = shape((rows, cols), BF16)
    wide = shape((rows, cols), F32)
    frame = shape((FT, cols), BF16)
    q_gain, k_gain = q_gain.reshape(1, cols), k_gain.reshape(1, cols)
    swap = [(h, (h + 1) % heads) for h in range(heads)]
    in_hbm = lambda x: pltpu.with_memory_space_constraint(x, pltpu.HBM)
    scores = lambda n: [pltpu.VMEM((cols // HD, rows, n), F32), pltpu.VMEM((cols // HD, rows, n), BF16)]

    sink_k, sink_v, both = call(
        lead_kernel, (frame, frame, shape((FT, 2 * cols), BF16)), (in_hbm(keys), in_hbm(values)),
        specs=[HBM, HBM], scratch=[pltpu.SemaphoreType.DMA((2,))],
    )
    near, far = call(
        pack_kernel,
        (shape((2 * FT, 2 * cols + LANES), BF16), shape((FT, 2 * cols + LANES), BF16)),
        (frames, keys, values), specs=[SMEM, VMEM, VMEM],
    )
    near = lax.ppermute(near, "tm", [(i, i + 1) for i in range(count - 1)])
    far = lax.ppermute(far, "tm", [(i, i + 2) for i in range(count - 2)])
    both = lax.ppermute(both, "tm", [(0, 1)])
    rounds = tree_rounds(count)
    for pairs, period in rounds:
        pairs = [pair for pair in pairs if pair != (0, 1)]
        came_k = lax.ppermute(sink_k, "tm", pairs)
        came_v = lax.ppermute(sink_v, "tm", pairs)
        kept = here % period == 0
        sink_k = jnp.where(kept, sink_k, came_k)
        sink_v = jnp.where(kept, sink_v, came_v)
    mine = call(sums_kernel, shape((rows, LANES), F32), (queries, keys))
    other = lax.ppermute(mine, "head", swap)
    ctl, qn, acc, top, den = call(
        lambda *refs: own_kernel(full_width, *refs), (shape((8, LANES), F32), block, wide, wide, wide),
        (frames, flags, queries, keys, values, q_gain, k_gain, mine, other), specs=[SMEM] + [VMEM] * 8,
        scratch=[pltpu.VMEM((rows, cols), BF16)] + scores(rows),
    )
    raw, mine = call(
        gather_kernel, (shape((3 * FT, cols), BF16), shape((3 * FT, LANES), F32)),
        (near, far, sink_k, both),
    )
    other = lax.ppermute(mine, "head", swap)
    return call(
        lambda *refs: finish_kernel(full_width, *refs), block,
        (frames, ctl, qn, raw, k_gain, mine, other, sink_v, both, near, far, acc, top, den),
        specs=[SMEM] + [VMEM] * 13,
        scratch=[pltpu.VMEM((3 * FT, cols), BF16)] + scores(3 * FT)
        + [pltpu.VMEM((cols // HD, rows, HD), F32)],
    )


def solution(mesh):
    placed = (
        P(("groups", "tm"), "head"),
        P(("groups", "tm"), "head"),
        P(("groups", "tm"), "head"),
        P("head"),
        P("head"),
        P(("groups", "tm")),
        P(("groups", "tm"), None),
    )
    return jax.shard_map(
        local, mesh=mesh, in_specs=placed, out_specs=P(("groups", "tm"), "head"), check_vma=False
    )
```

```python
import math

import jax
import jax.numpy as jnp
from jax import lax
from jax.experimental import pallas as pl
from jax.experimental.pallas import tpu as pltpu
from jax.sharding import PartitionSpec as P


HD = 128
FT = 32
EPSILON = 1e-06
LANES = 128
VMEM = pl.BlockSpec(memory_space=pltpu.VMEM)
HBM = pl.BlockSpec(memory_space=pltpu.HBM)
SMEM = pl.BlockSpec(memory_space=pltpu.SMEM)
PARAMS = pltpu.CompilerParams(vmem_limit_bytes=8 << 20)
F32 = jnp.float32
BF16 = jnp.bfloat16


def tree_rounds(count):
    stride = 1
    while stride * 2 < count:
        stride *= 2
    held, rounds = [0], []
    while stride:
        pairs = [(h, h + stride) for h in held if h + stride < count]
        rounds.append((pairs, 2 * stride))
        held = sorted(held + [target for _, target in pairs])
        stride //= 2
    return rounds


def call(kernel, shapes, operands, specs=None, scratch=(), out_specs=None):
    single = not isinstance(shapes, tuple)
    return pl.pallas_call(
        kernel,
        out_shape=shapes,
        in_specs=[VMEM] * len(operands) if specs is None else specs,
        out_specs=out_specs or (VMEM if single else (VMEM,) * len(shapes)),
        scratch_shapes=list(scratch),
        compiler_params=PARAMS,
    )(*operands)


def lead_kernel(k_hbm, v_hbm, sink_k_ref, sink_v_ref, sink_ref, sem):
    cols = k_hbm.shape[1]

    @pl.when(lax.axis_index("tm") == 0)
    def _():
        first = pltpu.make_async_copy(k_hbm.at[:FT, :], sink_k_ref, sem.at[0])
        second = pltpu.make_async_copy(v_hbm.at[:FT, :], sink_v_ref, sem.at[1])
        first.start()
        second.start()
        first.wait()
        second.wait()
        sink_ref[:, :cols] = sink_k_ref[...]
        sink_ref[:, cols:] = sink_v_ref[...]


def pack_kernel(frames_ref, k_ref, v_ref, near_ref, far_ref):
    rows, cols = k_ref.shape
    count = jnp.full((1, 1), frames_ref[0].astype(F32))
    counts = jnp.broadcast_to(count, (FT, cols))
    mark = jnp.broadcast_to(count, (FT, LANES)).astype(BF16)
    for ref, at in ((k_ref, 0), (v_ref, cols)):
        last, before = ref[:FT, :], ref[:FT, :]
        for frame in range(1, rows // FT):
            here = ref[frame * FT:(frame + 1) * FT, :]
            last = jnp.where(counts > frame + 0.5, here, last)
            before = jnp.where(counts > frame + 1.5, here, before)
        near_ref[:FT, at:at + cols] = last
        near_ref[FT:, at:at + cols] = before
        far_ref[:, at:at + cols] = last
    near_ref[:FT, 2 * cols:] = mark
    near_ref[FT:, 2 * cols:] = mark
    far_ref[:, 2 * cols:] = mark


def square_sums(ref):
    x = ref[...].astype(F32)
    return jnp.sum(x * x, axis=1, keepdims=True)


def sums_kernel(q_ref, k_ref, sums_ref):
    lane = lax.broadcasted_iota(jnp.int32, sums_ref.shape, 1)
    sums_ref[...] = jnp.where(lane < LANES // 2, square_sums(q_ref), square_sums(k_ref))


def own_kernel(full_width, frames_ref, flags_hbm, q_ref, k_ref, v_ref, qg_hbm, kg_hbm, mine_ref, other_ref,
               ctl_ref, gains_ref, qn_ref, acc_ref, top_ref, den_ref,
               kn_ref, score_ref, weight_ref, qg_ref, kg_ref, flags_ref, sem):
    rows, cols = q_ref.shape
    copies = [
        pltpu.make_async_copy(source, target, sem.at[i])
        for i, (source, target) in enumerate(((qg_hbm, qg_ref), (kg_hbm, kg_ref), (flags_hbm, flags_ref)))
    ]
    for copy in copies:
        copy.start()
    for copy in copies:
        copy.wait()
    row = lax.broadcasted_iota(jnp.int32, ctl_ref.shape, 0)
    ctl_ref[...] = jnp.where(row == 0, flags_ref[0, 0], flags_ref[0, 1]).astype(F32)
    gains_ref[:1, :] = qg_ref[...].reshape(1, cols)
    gains_ref[1:2, :] = kg_ref[...].reshape(1, cols)
    factor = lax.rsqrt((mine_ref[...] + other_ref[...]) / full_width + EPSILON)
    qn_ref[...] = (q_ref[...].astype(F32) * factor[:, :1] * gains_ref[:1, :]).astype(BF16)
    kn_ref[...] = (k_ref[...].astype(F32) * factor[:, LANES // 2:LANES // 2 + 1] * gains_ref[1:2, :]).astype(BF16)
    heads = [(i, i * HD, (i + 1) * HD) for i in range(cols // HD)]
    allowed = lax.broadcasted_iota(jnp.int32, (rows, rows), 1) < frames_ref[0] * FT
    ones = jnp.ones((rows, HD), BF16)
    for i, a, b in heads:
        score = lax.dot_general(
            qn_ref[:, a:b], kn_ref[:, a:b], (((1,), (1,)), ((), ())), preferred_element_type=F32
        ) * (1.0 / math.sqrt(HD))
        score_ref[i] = jnp.where(allowed, score, -jnp.inf)
    for i, a, b in heads:
        score = score_ref[i]
        top = jnp.max(score, axis=1, keepdims=True)
        top_ref[:, a:b] = jnp.broadcast_to(top, (rows, HD))
        weight_ref[i] = jnp.exp(score - top).astype(BF16)
    for i, a, b in heads:
        both = jnp.dot(weight_ref[i], jnp.concatenate([v_ref[:, a:b], ones], 1), preferred_element_type=F32)
        acc_ref[:, a:b] = both[:, :HD]
        den_ref[:, a:b] = both[:, HD:]


def gather_kernel(near_ref, far_ref, sink_k_ref, next_ref, gains_ref, keys_ref, sums_ref, raw_ref):
    cols = sink_k_ref.shape[1]
    pick = jnp.broadcast_to(near_ref[:1, 2 * cols:2 * cols + 1].astype(F32), (FT, cols)) > 1.5
    second = jnp.full((FT, cols), lax.axis_index("tm"), jnp.int32) == 1
    raw_ref[:FT, :] = near_ref[:FT, :cols]
    raw_ref[FT:2 * FT, :] = jnp.where(pick, near_ref[FT:, :cols], far_ref[:, :cols])
    raw_ref[2 * FT:, :] = jnp.where(second, next_ref[:, :cols], sink_k_ref[...])
    sums_ref[...] = jnp.zeros_like(sums_ref)
    sums_ref[:3 * FT, :] = jnp.broadcast_to(square_sums(raw_ref), (3 * FT, LANES))
    keys_ref[...] = (raw_ref[...].astype(F32) * gains_ref[1:2, :]).astype(BF16)


def score_kernel(q_ref, keys_ref, score_ref):
    for i in range(q_ref.shape[1] // HD):
        a, b = i * HD, (i + 1) * HD
        score_ref[i] = lax.dot_general(
            q_ref[:, a:b], keys_ref[:, a:b], (((1,), (1,)), ((), ())), preferred_element_type=F32
        )


def finish_kernel(full_width, frames_ref, ctl_ref, score_ref, mine_ref, other_ref, sink_v_ref, next_ref,
                  near_ref, far_ref, acc_ref, top_ref, den_ref, out_ref, weight_ref, keep_ref):
    rows, cols = out_ref.shape
    span = 3 * FT
    factor = lax.rsqrt((mine_ref[...] + other_ref[...]) / full_width + EPSILON) * (1.0 / math.sqrt(HD))
    factor = jnp.broadcast_to(jnp.transpose(factor)[:1, :span], (rows, span))
    heads = [(i, i * HD, (i + 1) * HD) for i in range(cols // HD)]
    sink = ctl_ref[:1, :1]
    window = ctl_ref[1:2, :1]
    near_mark = near_ref[:1, 2 * cols:2 * cols + 1].astype(F32)
    far_mark = far_ref[:1, 2 * cols:2 * cols + 1].astype(F32)
    has_before = jnp.where(near_mark > 1.5, near_mark, far_mark) * window
    slot = lax.broadcasted_iota(jnp.int32, (rows, span), 1)
    allow = jnp.where(slot < FT, near_mark * window, jnp.where(slot < 2 * FT, has_before, sink))
    allowed = allow > 0.5
    live = lax.broadcasted_iota(jnp.int32, (rows, HD), 0) < frames_ref[0] * FT
    pick = jnp.broadcast_to(near_mark, (FT, HD)) > 1.5
    second = jnp.full((FT, HD), lax.axis_index("tm"), jnp.int32) == 1
    ones = jnp.ones((span, HD), BF16)
    for i, a, b in heads:
        score = jnp.where(allowed, score_ref[i] * factor, -jnp.inf)
        old = top_ref[:, a:b]
        top = jnp.maximum(old, jnp.max(score, axis=1, keepdims=True))
        keep_ref[i] = jnp.exp(old - top)
        weight_ref[i] = jnp.exp(score - top[:, :span]).astype(BF16)
    for i, a, b in heads:
        c, d = cols + a, cols + b
        before = jnp.where(pick, near_ref[FT:, c:d], far_ref[:, c:d])
        first = jnp.where(second, next_ref[:, c:d], sink_v_ref[:, a:b])
        vals = jnp.concatenate([near_ref[:FT, c:d], before, first], 0)
        both = jnp.dot(weight_ref[i], jnp.concatenate([vals, ones], 1), preferred_element_type=F32)
        keep = keep_ref[i]
        blended = (acc_ref[:, a:b] * keep + both[:, :HD]) / (den_ref[:, a:b] * keep + both[:, HD:])
        out_ref[:, a:b] = jnp.where(live, blended, 0.0).astype(BF16)


def local(queries, keys, values, q_gain, k_gain, frames, flags):
    rows, cols = queries.shape
    heads = lax.axis_size("head")
    full_width = cols * heads
    count = lax.axis_size("tm")
    here = lax.axis_index("tm")
    shape = jax.ShapeDtypeStruct
    block = shape((rows, cols), BF16)
    wide = shape((rows, cols), F32)
    frame = shape((FT, cols), BF16)
    swap = [(h, (h + 1) % heads) for h in range(heads)]
    in_hbm = lambda x: pltpu.with_memory_space_constraint(x, pltpu.HBM)
    scores = lambda n: [pltpu.VMEM((cols // HD, rows, n), F32), pltpu.VMEM((cols // HD, rows, n), BF16)]

    sink_k, sink_v, both = call(
        lead_kernel, (frame, frame, shape((FT, 2 * cols), BF16)), (in_hbm(keys), in_hbm(values)),
        specs=[HBM, HBM], scratch=[pltpu.SemaphoreType.DMA((2,))],
    )
    near, far = call(
        pack_kernel,
        (shape((2 * FT, 2 * cols + LANES), BF16), shape((FT, 2 * cols + LANES), BF16)),
        (frames, keys, values), specs=[SMEM, VMEM, VMEM],
    )
    near = lax.ppermute(near, "tm", [(i, i + 1) for i in range(count - 1)])
    far = lax.ppermute(far, "tm", [(i, i + 2) for i in range(count - 2)])
    both = lax.ppermute(both, "tm", [(0, 1)])
    rounds = tree_rounds(count)
    for pairs, period in rounds:
        pairs = [pair for pair in pairs if pair != (0, 1)]
        came_k = lax.ppermute(sink_k, "tm", pairs)
        came_v = lax.ppermute(sink_v, "tm", pairs)
        kept = here % period == 0
        sink_k = jnp.where(kept, sink_k, came_k)
        sink_v = jnp.where(kept, sink_v, came_v)
    mine = call(sums_kernel, shape((rows, LANES), F32), (queries, keys))
    other = lax.ppermute(mine, "head", swap)
    ctl, gains, qn, acc, top, den = call(
        lambda *refs: own_kernel(full_width, *refs),
        (shape((8, LANES), F32), shape((8, cols), F32), block, wide, wide, wide),
        (
            frames, in_hbm(flags), queries, keys, values, in_hbm(q_gain), in_hbm(k_gain), mine, other,
        ),
        specs=[SMEM, HBM, VMEM, VMEM, VMEM, HBM, HBM, VMEM, VMEM],
        scratch=[pltpu.VMEM((rows, cols), BF16)] + scores(rows) + [
            pltpu.VMEM((cols,), F32), pltpu.VMEM((cols,), F32), pltpu.SMEM((1, 2), jnp.int32),
            pltpu.SemaphoreType.DMA((3,)),
        ],
    )
    keys, mine = call(
        gather_kernel, (shape((3 * FT, cols), BF16), shape((LANES, LANES), F32)),
        (near, far, sink_k, both, gains), scratch=[pltpu.VMEM((3 * FT, cols), BF16)],
    )
    other = lax.ppermute(mine, "head", swap)
    score = call(score_kernel, shape((cols // HD, rows, 3 * FT), F32), (qn, keys))
    return call(
        lambda *refs: finish_kernel(full_width, *refs), block,
        (frames, ctl, score, mine, other, sink_v, both, near, far, acc, top, den),
        specs=[SMEM] + [VMEM] * 11,
        scratch=[
            pltpu.VMEM((cols // HD, rows, 3 * FT), BF16), pltpu.VMEM((cols // HD, rows, HD), F32),
        ],
    )


def solution(mesh):
    placed = (
        P(("groups", "tm"), "head"),
        P(("groups", "tm"), "head"),
        P(("groups", "tm"), "head"),
        P("head"),
        P("head"),
        P(("groups", "tm")),
        P(("groups", "tm"), None),
    )
    return jax.shard_map(
        local, mesh=mesh, in_specs=placed, out_specs=P(("groups", "tm"), "head"), check_vma=False
    )
```

```python
import math

import jax
import jax.numpy as jnp
from jax import lax
from jax.experimental import pallas as pl
from jax.experimental.pallas import tpu as pltpu
from jax.sharding import PartitionSpec as P


HD = 128
FT = 32
EPSILON = 1e-06
LANES = 128
VMEM = pl.BlockSpec(memory_space=pltpu.VMEM)
HBM = pl.BlockSpec(memory_space=pltpu.HBM)
SMEM = pl.BlockSpec(memory_space=pltpu.SMEM)
PARAMS = pltpu.CompilerParams(vmem_limit_bytes=8 << 20)
F32 = jnp.float32
BF16 = jnp.bfloat16


def tree_rounds(count):
    stride = 1
    while stride * 2 < count:
        stride *= 2
    held, rounds = [0], []
    while stride:
        pairs = [(h, h + stride) for h in held if h + stride < count]
        rounds.append((pairs, 2 * stride))
        held = sorted(held + [target for _, target in pairs])
        stride //= 2
    return rounds


def call(kernel, shapes, operands, specs=None, scratch=(), out_specs=None):
    single = not isinstance(shapes, tuple)
    return pl.pallas_call(
        kernel,
        out_shape=shapes,
        in_specs=[VMEM] * len(operands) if specs is None else specs,
        out_specs=out_specs or (VMEM if single else (VMEM,) * len(shapes)),
        scratch_shapes=list(scratch),
        compiler_params=PARAMS,
    )(*operands)


def lead_kernel(k_hbm, v_hbm, sink_k_ref, sink_v_ref, sink_ref, sem):
    cols = k_hbm.shape[1]

    @pl.when(lax.axis_index("tm") == 0)
    def _():
        first = pltpu.make_async_copy(k_hbm.at[:FT, :], sink_k_ref, sem.at[0])
        second = pltpu.make_async_copy(v_hbm.at[:FT, :], sink_v_ref, sem.at[1])
        first.start()
        second.start()
        first.wait()
        second.wait()
        sink_ref[:, :cols] = sink_k_ref[...]
        sink_ref[:, cols:] = sink_v_ref[...]


def pack_kernel(frames_ref, k_ref, v_ref, near_ref, far_ref):
    rows, cols = k_ref.shape
    count = jnp.full((1, 1), frames_ref[0].astype(F32))
    counts = jnp.broadcast_to(count, (FT, cols))
    mark = jnp.broadcast_to(count, (FT, LANES)).astype(BF16)
    for ref, at in ((k_ref, 0), (v_ref, cols)):
        last, before = ref[:FT, :], ref[:FT, :]
        for frame in range(1, rows // FT):
            here = ref[frame * FT:(frame + 1) * FT, :]
            last = jnp.where(counts > frame + 0.5, here, last)
            before = jnp.where(counts > frame + 1.5, here, before)
        near_ref[:FT, at:at + cols] = last
        near_ref[FT:, at:at + cols] = before
        far_ref[:, at:at + cols] = last
    near_ref[:FT, 2 * cols:] = mark
    near_ref[FT:, 2 * cols:] = mark
    far_ref[:, 2 * cols:] = mark


def square_sums(ref):
    x = ref[...].astype(F32)
    return jnp.sum(x * x, axis=1, keepdims=True)


def sums_kernel(q_ref, k_ref, sums_ref):
    lane = lax.broadcasted_iota(jnp.int32, sums_ref.shape, 1)
    sums_ref[...] = jnp.where(lane < LANES // 2, square_sums(q_ref), square_sums(k_ref))


def own_kernel(full_width, frames_ref, flags_hbm, q_ref, k_ref, v_ref, qg_hbm, kg_hbm, mine_ref, other_ref,
               ctl_ref, gains_ref, qn_ref, acc_ref, top_ref, den_ref,
               kn_ref, score_ref, weight_ref, qg_ref, kg_ref, flags_ref, sem):
    rows, cols = q_ref.shape
    copies = [
        pltpu.make_async_copy(source, target, sem.at[i])
        for i, (source, target) in enumerate(((qg_hbm, qg_ref), (kg_hbm, kg_ref), (flags_hbm, flags_ref)))
    ]
    for copy in copies:
        copy.start()
    for copy in copies:
        copy.wait()
    row = lax.broadcasted_iota(jnp.int32, ctl_ref.shape, 0)
    ctl_ref[...] = jnp.where(row == 0, flags_ref[0, 0], flags_ref[0, 1]).astype(F32)
    gains_ref[:1, :] = qg_ref[...].reshape(1, cols)
    gains_ref[1:2, :] = kg_ref[...].reshape(1, cols)
    factor = lax.rsqrt((mine_ref[...] + other_ref[...]) / full_width + EPSILON)
    qn_ref[...] = (q_ref[...].astype(F32) * factor[:, :1] * gains_ref[:1, :]).astype(BF16)
    kn_ref[...] = (k_ref[...].astype(F32) * factor[:, LANES // 2:LANES // 2 + 1] * gains_ref[1:2, :]).astype(BF16)
    heads = [(i, i * HD, (i + 1) * HD) for i in range(cols // HD)]
    allowed = lax.broadcasted_iota(jnp.int32, (rows, rows), 1) < frames_ref[0] * FT
    ones = jnp.ones((rows, HD), BF16)
    for i, a, b in heads:
        score = lax.dot_general(
            qn_ref[:, a:b], kn_ref[:, a:b], (((1,), (1,)), ((), ())), preferred_element_type=F32
        ) * (1.0 / math.sqrt(HD))
        score_ref[i] = jnp.where(allowed, score, -jnp.inf)
    for i, a, b in heads:
        score = score_ref[i]
        top = jnp.max(score, axis=1, keepdims=True)
        top_ref[:, a:b] = jnp.broadcast_to(top, (rows, HD))
        weight_ref[i] = jnp.exp(score - top).astype(BF16)
    for i, a, b in heads:
        both = jnp.dot(weight_ref[i], jnp.concatenate([v_ref[:, a:b], ones], 1), preferred_element_type=F32)
        acc_ref[:, a:b] = both[:, :HD]
        den_ref[:, a:b] = both[:, HD:]


def gather_kernel(near_ref, far_ref, sink_k_ref, next_ref, keys_ref, sums_ref):
    cols = sink_k_ref.shape[1]
    pick = jnp.broadcast_to(near_ref[:1, 2 * cols:2 * cols + 1].astype(F32), (FT, cols)) > 1.5
    second = jnp.full((FT, cols), lax.axis_index("tm"), jnp.int32) == 1
    keys_ref[:FT, :] = near_ref[:FT, :cols]
    keys_ref[FT:2 * FT, :] = jnp.where(pick, near_ref[FT:, :cols], far_ref[:, :cols])
    keys_ref[2 * FT:, :] = jnp.where(second, next_ref[:, :cols], sink_k_ref[...])
    sums = jnp.broadcast_to(square_sums(keys_ref), (3 * FT, LANES))
    square = jnp.concatenate([sums, jnp.zeros((LANES - 3 * FT, LANES), F32)], 0)
    sums_ref[...] = jnp.transpose(square)[:8, :]


def score_kernel(q_ref, keys_ref, gains_ref, score_ref, high_ref, low_ref):
    scaled = keys_ref[...].astype(F32) * gains_ref[1:2, :]
    high_ref[...] = scaled.astype(BF16)
    low_ref[...] = (scaled - high_ref[...].astype(F32)).astype(BF16)
    for i in range(q_ref.shape[1] // HD):
        a, b = i * HD, (i + 1) * HD
        score_ref[i] = lax.dot_general(
            jnp.concatenate([q_ref[:, a:b], q_ref[:, a:b]], 1), jnp.concatenate([high_ref[:, a:b], low_ref[:, a:b]], 1),
            (((1,), (1,)), ((), ())), preferred_element_type=F32,
        )


def finish_kernel(full_width, frames_ref, ctl_ref, score_ref, mine_ref, other_ref, sink_v_ref, next_ref,
                  near_ref, far_ref, acc_ref, top_ref, den_ref, out_hbm, weight_ref, keep_ref, out_ref, sem):
    rows, cols = out_ref.shape
    span = 3 * FT
    factor = lax.rsqrt((mine_ref[...] + other_ref[...]) / full_width + EPSILON) * (1.0 / math.sqrt(HD))
    factor = jnp.broadcast_to(factor[:1, :span], (rows, span))
    heads = [(i, i * HD, (i + 1) * HD) for i in range(cols // HD)]
    sink = ctl_ref[:1, :1]
    window = ctl_ref[1:2, :1]
    near_mark = near_ref[:1, 2 * cols:2 * cols + 1].astype(F32)
    far_mark = far_ref[:1, 2 * cols:2 * cols + 1].astype(F32)
    has_before = jnp.where(near_mark > 1.5, near_mark, far_mark) * window
    slot = lax.broadcasted_iota(jnp.int32, (rows, span), 1)
    allow = jnp.where(slot < FT, near_mark * window, jnp.where(slot < 2 * FT, has_before, sink))
    allowed = allow > 0.5
    live = lax.broadcasted_iota(jnp.int32, (rows, HD), 0) < frames_ref[0] * FT
    pick = jnp.broadcast_to(near_mark, (FT, HD)) > 1.5
    second = jnp.full((FT, HD), lax.axis_index("tm"), jnp.int32) == 1
    ones = jnp.ones((span, HD), BF16)
    for i, a, b in heads:
        score = jnp.where(allowed, score_ref[i] * factor, -jnp.inf)
        old = top_ref[:, a:b]
        top = jnp.maximum(old, jnp.max(score, axis=1, keepdims=True))
        keep_ref[i] = jnp.exp(old - top)
        weight_ref[i] = jnp.exp(score - top[:, :span]).astype(BF16)
    half = (len(heads) + 1) // 2
    copies = [
        pltpu.make_async_copy(out_ref.at[:, a:b], out_hbm.at[:, a:b], sem.at[n])
        for n, (a, b) in enumerate(((0, half * HD), (half * HD, cols))) if a < b
    ]
    for i, a, b in heads:
        c, d = cols + a, cols + b
        before = jnp.where(pick, near_ref[FT:, c:d], far_ref[:, c:d])
        first = jnp.where(second, next_ref[:, c:d], sink_v_ref[:, a:b])
        vals = jnp.concatenate([near_ref[:FT, c:d], before, first], 0)
        both = jnp.dot(weight_ref[i], jnp.concatenate([vals, ones], 1), preferred_element_type=F32)
        keep = keep_ref[i]
        blended = (acc_ref[:, a:b] * keep + both[:, :HD]) / (den_ref[:, a:b] * keep + both[:, HD:])
        out_ref[:, a:b] = jnp.where(live, blended, 0.0).astype(BF16)
        if i == half - 1:
            copies[0].start()
    for copy in copies[1:]:
        copy.start()
    for copy in copies:
        copy.wait()


def local(queries, keys, values, q_gain, k_gain, frames, flags):
    rows, cols = queries.shape
    heads = lax.axis_size("head")
    full_width = cols * heads
    count = lax.axis_size("tm")
    here = lax.axis_index("tm")
    shape = jax.ShapeDtypeStruct
    block = shape((rows, cols), BF16)
    wide = shape((rows, cols), F32)
    frame = shape((FT, cols), BF16)
    swap = [(h, (h + 1) % heads) for h in range(heads)]
    in_hbm = lambda x: pltpu.with_memory_space_constraint(x, pltpu.HBM)
    scores = lambda n: [pltpu.VMEM((cols // HD, rows, n), F32), pltpu.VMEM((cols // HD, rows, n), BF16)]

    sink_k, sink_v, both = call(
        lead_kernel, (frame, frame, shape((FT, 2 * cols), BF16)), (in_hbm(keys), in_hbm(values)),
        specs=[HBM, HBM], scratch=[pltpu.SemaphoreType.DMA((2,))],
    )
    near, far = call(
        pack_kernel,
        (shape((2 * FT, 2 * cols + LANES), BF16), shape((FT, 2 * cols + LANES), BF16)),
        (frames, keys, values), specs=[SMEM, VMEM, VMEM],
    )
    near = lax.ppermute(near, "tm", [(i, i + 1) for i in range(count - 1)])
    far = lax.ppermute(far, "tm", [(i, i + 2) for i in range(count - 2)])
    both = lax.ppermute(both, "tm", [(0, 1)])
    rounds = tree_rounds(count)
    for pairs, period in rounds:
        pairs = [pair for pair in pairs if pair != (0, 1)]
        came_k = lax.ppermute(sink_k, "tm", pairs)
        came_v = lax.ppermute(sink_v, "tm", pairs)
        kept = here % period == 0
        sink_k = jnp.where(kept, sink_k, came_k)
        sink_v = jnp.where(kept, sink_v, came_v)
    mine = call(sums_kernel, shape((rows, LANES), F32), (queries, keys))
    other = lax.ppermute(mine, "head", swap)
    ctl, gains, qn, acc, top, den = call(
        lambda *refs: own_kernel(full_width, *refs),
        (shape((8, LANES), F32), shape((8, cols), F32), block, wide, wide, wide),
        (
            frames, in_hbm(flags), queries, keys, values, in_hbm(q_gain), in_hbm(k_gain), mine, other,
        ),
        specs=[SMEM, HBM, VMEM, VMEM, VMEM, HBM, HBM, VMEM, VMEM],
        scratch=[pltpu.VMEM((rows, cols), BF16)] + scores(rows) + [
            pltpu.VMEM((cols,), F32), pltpu.VMEM((cols,), F32), pltpu.SMEM((1, 2), jnp.int32),
            pltpu.SemaphoreType.DMA((3,)),
        ],
    )
    keys, mine = call(gather_kernel, (shape((3 * FT, cols), BF16), shape((8, LANES), F32)), (near, far, sink_k, both))
    other = lax.ppermute(mine, "head", swap)
    score = call(
        score_kernel, shape((cols // HD, rows, 3 * FT), F32), (qn, keys, gains),
        scratch=[pltpu.VMEM((3 * FT, cols), BF16)] * 2,
    )
    return call(
        lambda *refs: finish_kernel(full_width, *refs), block,
        (frames, ctl, score, mine, other, sink_v, both, near, far, acc, top, den),
        specs=[SMEM] + [VMEM] * 11,
        scratch=[
            pltpu.VMEM((cols // HD, rows, 3 * FT), BF16), pltpu.VMEM((cols // HD, rows, HD), F32),
            pltpu.VMEM((rows, cols), BF16), pltpu.SemaphoreType.DMA((2,)),
        ],
        out_specs=HBM,
    )


def solution(mesh):
    placed = (
        P(("groups", "tm"), "head"),
        P(("groups", "tm"), "head"),
        P(("groups", "tm"), "head"),
        P("head"),
        P("head"),
        P(("groups", "tm")),
        P(("groups", "tm"), None),
    )
    return jax.shard_map(
        local, mesh=mesh, in_specs=placed, out_specs=P(("groups", "tm"), "head"), check_vma=False
    )
```

```python
import math

import jax
import jax.numpy as jnp
from jax import lax
from jax.experimental import pallas as pl
from jax.experimental.pallas import tpu as pltpu
from jax.sharding import PartitionSpec as P


HD = 128
FT = 32
EPSILON = 1e-06
LANES = 128
MISSING = 4096.0
VMEM = pl.BlockSpec(memory_space=pltpu.VMEM)
HBM = pl.BlockSpec(memory_space=pltpu.HBM)
SMEM = pl.BlockSpec(memory_space=pltpu.SMEM)
PARAMS = pltpu.CompilerParams(vmem_limit_bytes=8 << 20)
F32 = jnp.float32
BF16 = jnp.bfloat16


def tree_rounds(count):
    stride = 1
    while stride * 2 < count:
        stride *= 2
    held, rounds = [0], []
    while stride:
        pairs = [(h, h + stride) for h in held if h + stride < count]
        rounds.append((pairs, 2 * stride))
        held = sorted(held + [target for _, target in pairs])
        stride //= 2
    return rounds


def call(kernel, shapes, operands, specs=None, scratch=(), out_specs=None):
    single = not isinstance(shapes, tuple)
    return pl.pallas_call(
        kernel,
        out_shape=shapes,
        in_specs=[VMEM] * len(operands) if specs is None else specs,
        out_specs=out_specs or (VMEM if single else (VMEM,) * len(shapes)),
        scratch_shapes=list(scratch),
        compiler_params=PARAMS,
    )(*operands)


def lead_kernel(k_hbm, v_hbm, sink_k_ref, sink_v_ref, sink_ref, sem):
    cols = k_hbm.shape[1]

    @pl.when(lax.axis_index("tm") == 0)
    def _():
        first = pltpu.make_async_copy(k_hbm.at[:FT, :], sink_k_ref, sem.at[0])
        second = pltpu.make_async_copy(v_hbm.at[:FT, :], sink_v_ref, sem.at[1])
        first.start()
        second.start()
        first.wait()
        second.wait()
        sink_ref[:, :cols] = sink_k_ref[...]
        sink_ref[:, cols:] = sink_v_ref[...]


def pack_kernel(frames_ref, k_ref, v_ref, near_ref, far_ref):
    rows, cols = k_ref.shape
    count = jnp.full((1, 1), frames_ref[0].astype(F32))
    counts = jnp.broadcast_to(count, (FT, cols))
    for ref, at in ((k_ref, 0), (v_ref, cols)):
        last, before = ref[:FT, :], ref[:FT, :]
        for frame in range(1, rows // FT):
            here = ref[frame * FT:(frame + 1) * FT, :]
            last = jnp.where(counts > frame + 0.5, here, last)
            before = jnp.where(counts > frame + 1.5, here, before)
        near_ref[:FT, at:at + cols] = last
        near_ref[FT:, at:at + cols] = before
        far_ref[:, at:at + cols] = last
    near_ref[FT:, :cols] = jnp.where(counts > 1.5, near_ref[FT:, :cols], jnp.full((FT, cols), MISSING, BF16))


def square_sums(ref):
    x = ref[...].astype(F32)
    return jnp.sum(x * x, axis=1, keepdims=True)


def sums_kernel(q_ref, k_ref, sums_ref):
    lane = lax.broadcasted_iota(jnp.int32, sums_ref.shape, 1)
    sums_ref[...] = jnp.where(lane < LANES // 2, square_sums(q_ref), square_sums(k_ref))


def own_kernel(full_width, frames_ref, flags_hbm, q_ref, k_ref, v_ref, qg_hbm, kg_hbm, mine_ref, other_ref,
               ctl_ref, gains_ref, qn_ref, acc_ref, top_ref, den_ref,
               kn_ref, score_ref, weight_ref, qg_ref, kg_ref, flags_ref, sem):
    rows, cols = q_ref.shape
    copies = [
        pltpu.make_async_copy(source, target, sem.at[i])
        for i, (source, target) in enumerate(((qg_hbm, qg_ref), (kg_hbm, kg_ref), (flags_hbm, flags_ref)))
    ]
    for copy in copies:
        copy.start()
    for copy in copies:
        copy.wait()
    row = lax.broadcasted_iota(jnp.int32, ctl_ref.shape, 0)
    ctl_ref[...] = jnp.where(row == 0, flags_ref[0, 0], flags_ref[0, 1]).astype(F32)
    gains_ref[:1, :] = qg_ref[...].reshape(1, cols)
    gains_ref[1:2, :] = kg_ref[...].reshape(1, cols)
    factor = lax.rsqrt((mine_ref[...] + other_ref[...]) / full_width + EPSILON)
    qn_ref[...] = (q_ref[...].astype(F32) * factor[:, :1] * gains_ref[:1, :]).astype(BF16)
    kn_ref[...] = (k_ref[...].astype(F32) * factor[:, LANES // 2:LANES // 2 + 1] * gains_ref[1:2, :]).astype(BF16)
    heads = [(i, i * HD, (i + 1) * HD) for i in range(cols // HD)]
    allowed = lax.broadcasted_iota(jnp.int32, (rows, rows), 1) < frames_ref[0] * FT
    ones = jnp.ones((rows, HD), BF16)
    for i, a, b in heads:
        score = lax.dot_general(
            qn_ref[:, a:b], kn_ref[:, a:b], (((1,), (1,)), ((), ())), preferred_element_type=F32
        ) * (1.0 / math.sqrt(HD))
        score_ref[i] = jnp.where(allowed, score, -jnp.inf)
    for i, a, b in heads:
        score = score_ref[i]
        top = jnp.max(score, axis=1, keepdims=True)
        top_ref[:, a:b] = jnp.broadcast_to(top, (rows, HD))
        weight_ref[i] = jnp.exp(score - top).astype(BF16)
    for i, a, b in heads:
        both = jnp.dot(weight_ref[i], jnp.concatenate([v_ref[:, a:b], ones], 1), preferred_element_type=F32)
        acc_ref[:, a:b] = both[:, :HD]
        den_ref[:, a:b] = both[:, HD:]


def gather_kernel(near_ref, far_ref, sink_k_ref, next_ref, keys_ref, sums_ref):
    cols = sink_k_ref.shape[1]
    pick = jnp.broadcast_to(near_ref[FT:FT + 1, :1].astype(F32), (FT, cols)) < MISSING / 2
    second = jnp.full((FT, cols), lax.axis_index("tm"), jnp.int32) == 1
    keys_ref[:FT, :] = near_ref[:FT, :cols]
    keys_ref[FT:2 * FT, :] = jnp.where(pick, near_ref[FT:, :cols], far_ref[:, :cols])
    keys_ref[2 * FT:, :] = jnp.where(second, next_ref[:, :cols], sink_k_ref[...])
    sums = jnp.broadcast_to(square_sums(keys_ref), (3 * FT, LANES))
    square = jnp.concatenate([sums, jnp.zeros((LANES - 3 * FT, LANES), F32)], 0)
    sums_ref[...] = jnp.transpose(square)[:8, :]


def score_kernel(q_ref, keys_ref, gains_ref, score_ref, high_ref, low_ref):
    scaled = keys_ref[...].astype(F32) * gains_ref[1:2, :]
    high_ref[...] = scaled.astype(BF16)
    low_ref[...] = (scaled - high_ref[...].astype(F32)).astype(BF16)
    for i in range(q_ref.shape[1] // HD):
        a, b = i * HD, (i + 1) * HD
        score_ref[i] = lax.dot_general(
            jnp.concatenate([q_ref[:, a:b], q_ref[:, a:b]], 1), jnp.concatenate([high_ref[:, a:b], low_ref[:, a:b]], 1),
            (((1,), (1,)), ((), ())), preferred_element_type=F32,
        )


def finish_kernel(full_width, frames_ref, ctl_ref, score_ref, mine_ref, other_ref, sink_v_ref, next_ref,
                  near_ref, far_ref, acc_ref, top_ref, den_ref, out_hbm, weight_ref, keep_ref, out_ref, sem):
    rows, cols = out_ref.shape
    span = 3 * FT
    factor = lax.rsqrt((mine_ref[...] + other_ref[...]) / full_width + EPSILON) * (1.0 / math.sqrt(HD))
    factor = jnp.broadcast_to(factor[:1, :span], (rows, span))
    heads = [(i, i * HD, (i + 1) * HD) for i in range(cols // HD)]
    sink = ctl_ref[:1, :1]
    window = ctl_ref[1:2, :1]
    here = lax.axis_index("tm")
    two = near_ref[FT:FT + 1, :1].astype(F32)
    has_last = jnp.where(jnp.full((1, 1), here, jnp.int32) > 0, window, 0.0)
    has_before = jnp.where((two < MISSING / 2) | (jnp.full((1, 1), here, jnp.int32) > 1), has_last, 0.0)
    slot = lax.broadcasted_iota(jnp.int32, (rows, span), 1)
    allow = jnp.where(slot < FT, has_last, jnp.where(slot < 2 * FT, has_before, sink))
    allowed = allow > 0.5
    live = lax.broadcasted_iota(jnp.int32, (rows, HD), 0) < frames_ref[0] * FT
    pick = jnp.broadcast_to(two, (FT, HD)) < MISSING / 2
    second = jnp.full((FT, HD), here, jnp.int32) == 1
    ones = jnp.ones((span, HD), BF16)
    for i, a, b in heads:
        score = jnp.where(allowed, score_ref[i] * factor, -jnp.inf)
        old = top_ref[:, a:b]
        top = jnp.maximum(old, jnp.max(score, axis=1, keepdims=True))
        keep_ref[i] = jnp.exp(old - top)
        weight_ref[i] = jnp.exp(score - top[:, :span]).astype(BF16)
    half = (len(heads) + 1) // 2
    copies = [
        pltpu.make_async_copy(out_ref.at[:, a:b], out_hbm.at[:, a:b], sem.at[n])
        for n, (a, b) in enumerate(((0, half * HD), (half * HD, cols))) if a < b
    ]
    for i, a, b in heads:
        c, d = cols + a, cols + b
        before = jnp.where(pick, near_ref[FT:, c:d], far_ref[:, c:d])
        first = jnp.where(second, next_ref[:, c:d], sink_v_ref[:, a:b])
        vals = jnp.concatenate([near_ref[:FT, c:d], before, first], 0)
        both = jnp.dot(weight_ref[i], jnp.concatenate([vals, ones], 1), preferred_element_type=F32)
        keep = keep_ref[i]
        blended = (acc_ref[:, a:b] * keep + both[:, :HD]) / (den_ref[:, a:b] * keep + both[:, HD:])
        out_ref[:, a:b] = jnp.where(live, blended, 0.0).astype(BF16)
        if i == half - 1:
            copies[0].start()
    for copy in copies[1:]:
        copy.start()
    for copy in copies:
        copy.wait()


def local(queries, keys, values, q_gain, k_gain, frames, flags):
    rows, cols = queries.shape
    heads = lax.axis_size("head")
    full_width = cols * heads
    count = lax.axis_size("tm")
    here = lax.axis_index("tm")
    shape = jax.ShapeDtypeStruct
    block = shape((rows, cols), BF16)
    wide = shape((rows, cols), F32)
    frame = shape((FT, cols), BF16)
    swap = [(h, (h + 1) % heads) for h in range(heads)]
    in_hbm = lambda x: pltpu.with_memory_space_constraint(x, pltpu.HBM)
    scores = lambda n: [pltpu.VMEM((cols // HD, rows, n), F32), pltpu.VMEM((cols // HD, rows, n), BF16)]

    sink_k, sink_v, both = call(
        lead_kernel, (frame, frame, shape((FT, 2 * cols), BF16)), (in_hbm(keys), in_hbm(values)),
        specs=[HBM, HBM], scratch=[pltpu.SemaphoreType.DMA((2,))],
    )
    near, far = call(
        pack_kernel,
        (shape((2 * FT, 2 * cols), BF16), shape((FT, 2 * cols), BF16)),
        (frames, keys, values), specs=[SMEM, VMEM, VMEM],
    )
    near = lax.ppermute(near, "tm", [(i, i + 1) for i in range(count - 1)])
    far = lax.ppermute(far, "tm", [(i, i + 2) for i in range(count - 2)])
    both = lax.ppermute(both, "tm", [(0, 1)])
    rounds = tree_rounds(count)
    for pairs, period in rounds:
        pairs = [pair for pair in pairs if pair != (0, 1)]
        came_k = lax.ppermute(sink_k, "tm", pairs)
        came_v = lax.ppermute(sink_v, "tm", pairs)
        kept = here % period == 0
        sink_k = jnp.where(kept, sink_k, came_k)
        sink_v = jnp.where(kept, sink_v, came_v)
    mine = call(sums_kernel, shape((rows, LANES), F32), (queries, keys))
    other = lax.ppermute(mine, "head", swap)
    ctl, gains, qn, acc, top, den = call(
        lambda *refs: own_kernel(full_width, *refs),
        (shape((8, LANES), F32), shape((8, cols), F32), block, wide, wide, wide),
        (
            frames, in_hbm(flags), queries, keys, values, in_hbm(q_gain), in_hbm(k_gain), mine, other,
        ),
        specs=[SMEM, HBM, VMEM, VMEM, VMEM, HBM, HBM, VMEM, VMEM],
        scratch=[pltpu.VMEM((rows, cols), BF16)] + scores(rows) + [
            pltpu.VMEM((cols,), F32), pltpu.VMEM((cols,), F32), pltpu.SMEM((1, 2), jnp.int32),
            pltpu.SemaphoreType.DMA((3,)),
        ],
    )
    keys, mine = call(gather_kernel, (shape((3 * FT, cols), BF16), shape((8, LANES), F32)), (near, far, sink_k, both))
    other = lax.ppermute(mine, "head", swap)
    score = call(
        score_kernel, shape((cols // HD, rows, 3 * FT), F32), (qn, keys, gains),
        scratch=[pltpu.VMEM((3 * FT, cols), BF16)] * 2,
    )
    return call(
        lambda *refs: finish_kernel(full_width, *refs), block,
        (frames, ctl, score, mine, other, sink_v, both, near, far, acc, top, den),
        specs=[SMEM] + [VMEM] * 11,
        scratch=[
            pltpu.VMEM((cols // HD, rows, 3 * FT), BF16), pltpu.VMEM((cols // HD, rows, HD), F32),
            pltpu.VMEM((rows, cols), BF16), pltpu.SemaphoreType.DMA((2,)),
        ],
        out_specs=HBM,
    )


def solution(mesh):
    placed = (
        P(("groups", "tm"), "head"),
        P(("groups", "tm"), "head"),
        P(("groups", "tm"), "head"),
        P("head"),
        P("head"),
        P(("groups", "tm")),
        P(("groups", "tm"), None),
    )
    return jax.shard_map(
        local, mesh=mesh, in_specs=placed, out_specs=P(("groups", "tm"), "head"), check_vma=False
    )
```

```python
import math

import jax
import jax.numpy as jnp
from jax import lax
from jax.experimental import pallas as pl
from jax.experimental.pallas import tpu as pltpu
from jax.sharding import PartitionSpec as P


HD = 128
FT = 32
EPSILON = 1e-06
LANES = 128
MISSING = 4096.0
VMEM = pl.BlockSpec(memory_space=pltpu.VMEM)
HBM = pl.BlockSpec(memory_space=pltpu.HBM)
SMEM = pl.BlockSpec(memory_space=pltpu.SMEM)
PARAMS = pltpu.CompilerParams(vmem_limit_bytes=8 << 20)
F32 = jnp.float32
BF16 = jnp.bfloat16


def tree_rounds(count):
    stride = 1
    while stride * 2 < count:
        stride *= 2
    held, rounds = [0], []
    while stride:
        pairs = [(h, h + stride) for h in held if h + stride < count]
        rounds.append((pairs, 2 * stride))
        held = sorted(held + [target for _, target in pairs])
        stride //= 2
    return rounds


def call(kernel, shapes, operands, specs=None, scratch=(), out_specs=None):
    single = not isinstance(shapes, tuple)
    return pl.pallas_call(
        kernel,
        out_shape=shapes,
        in_specs=[VMEM] * len(operands) if specs is None else specs,
        out_specs=out_specs or (VMEM if single else (VMEM,) * len(shapes)),
        scratch_shapes=list(scratch),
        compiler_params=PARAMS,
    )(*operands)


def lead_kernel(k_hbm, v_hbm, sink_k_ref, sink_v_ref, sink_ref, sem):
    cols = k_hbm.shape[1]

    @pl.when(lax.axis_index("tm") == 0)
    def _():
        first = pltpu.make_async_copy(k_hbm.at[:FT, :], sink_k_ref, sem.at[0])
        second = pltpu.make_async_copy(v_hbm.at[:FT, :], sink_v_ref, sem.at[1])
        first.start()
        second.start()
        first.wait()
        second.wait()
        sink_ref[:, :cols] = sink_k_ref[...]
        sink_ref[:, cols:] = sink_v_ref[...]


def pack_kernel(frames_ref, k_ref, v_ref, near_ref, far_ref):
    rows, cols = k_ref.shape
    count = jnp.full((1, 1), frames_ref[0].astype(F32))
    counts = jnp.broadcast_to(count, (FT, cols))
    for ref, at in ((k_ref, 0), (v_ref, cols)):
        last, before = ref[:FT, :], ref[:FT, :]
        for frame in range(1, rows // FT):
            here = ref[frame * FT:(frame + 1) * FT, :]
            last = jnp.where(counts > frame + 0.5, here, last)
            before = jnp.where(counts > frame + 1.5, here, before)
        near_ref[:FT, at:at + cols] = last
        near_ref[FT:, at:at + cols] = before
        far_ref[:, at:at + cols] = last
    near_ref[FT:, :cols] = jnp.where(counts > 1.5, near_ref[FT:, :cols], jnp.full((FT, cols), MISSING, BF16))


def square_sums(ref):
    x = ref[...].astype(F32)
    return jnp.sum(x * x, axis=1, keepdims=True)


def sums_kernel(q_ref, k_ref, sums_ref):
    lane = lax.broadcasted_iota(jnp.int32, sums_ref.shape, 1)
    sums_ref[...] = jnp.where(lane < LANES // 2, square_sums(q_ref), square_sums(k_ref))


def own_kernel(full_width, frames_ref, flags_hbm, q_ref, k_ref, v_ref, qg_hbm, kg_hbm, mine_ref, other_ref,
               ctl_ref, gains_ref, qn_ref, acc_ref, top_ref, den_ref,
               kn_ref, score_ref, weight_ref, qg_ref, kg_ref, flags_ref, sem):
    rows, cols = q_ref.shape
    copies = [
        pltpu.make_async_copy(source, target, sem.at[i])
        for i, (source, target) in enumerate(((qg_hbm, qg_ref), (kg_hbm, kg_ref), (flags_hbm, flags_ref)))
    ]
    for copy in copies:
        copy.start()
    for copy in copies:
        copy.wait()
    row = lax.broadcasted_iota(jnp.int32, ctl_ref.shape, 0)
    ctl_ref[...] = jnp.where(row == 0, flags_ref[0, 0], flags_ref[0, 1]).astype(F32)
    gains_ref[:1, :] = qg_ref[...].reshape(1, cols)
    gains_ref[1:2, :] = kg_ref[...].reshape(1, cols)
    factor = lax.rsqrt((mine_ref[...] + other_ref[...]) / full_width + EPSILON)
    qn_ref[...] = (q_ref[...].astype(F32) * factor[:, :1] * gains_ref[:1, :]).astype(BF16)
    kn_ref[...] = (k_ref[...].astype(F32) * factor[:, LANES // 2:LANES // 2 + 1] * gains_ref[1:2, :]).astype(BF16)
    heads = [(i, i * HD, (i + 1) * HD) for i in range(cols // HD)]
    allowed = lax.broadcasted_iota(jnp.int32, (rows, rows), 1) < frames_ref[0] * FT
    ones = jnp.ones((rows, HD), BF16)
    for i, a, b in heads:
        score = lax.dot_general(
            qn_ref[:, a:b], kn_ref[:, a:b], (((1,), (1,)), ((), ())), preferred_element_type=F32
        ) * (1.0 / math.sqrt(HD))
        score_ref[i] = jnp.where(allowed, score, -jnp.inf)
    for i, a, b in heads:
        score = score_ref[i]
        top = jnp.max(score, axis=1, keepdims=True)
        top_ref[:, a:b] = jnp.broadcast_to(top, (rows, HD))
        weight_ref[i] = jnp.exp(score - top).astype(BF16)
    for i, a, b in heads:
        both = jnp.dot(weight_ref[i], jnp.concatenate([v_ref[:, a:b], ones], 1), preferred_element_type=F32)
        acc_ref[:, a:b] = both[:, :HD]
        den_ref[:, a:b] = both[:, HD:]


def gather_kernel(near_ref, far_ref, sink_k_ref, came_k_ref, next_ref, keys_ref, sums_ref):
    cols = sink_k_ref.shape[1]
    pick = jnp.broadcast_to(near_ref[FT:FT + 1, :1].astype(F32), (FT, cols)) < MISSING / 2
    here = jnp.full((FT, cols), lax.axis_index("tm"), jnp.int32)
    keys_ref[:FT, :] = near_ref[:FT, :cols]
    keys_ref[FT:2 * FT, :] = jnp.where(pick, near_ref[FT:, :cols], far_ref[:, :cols])
    came = jnp.where(here == 1, next_ref[:, :cols], came_k_ref[...])
    keys_ref[2 * FT:, :] = jnp.where(here % 2 == 0, sink_k_ref[...], came)
    sums = jnp.broadcast_to(square_sums(keys_ref), (3 * FT, LANES))
    square = jnp.concatenate([sums, jnp.zeros((LANES - 3 * FT, LANES), F32)], 0)
    sums_ref[...] = jnp.transpose(square)[:8, :]


def score_kernel(q_ref, keys_ref, gains_ref, score_ref, high_ref, low_ref):
    scaled = keys_ref[...].astype(F32) * gains_ref[1:2, :]
    high_ref[...] = scaled.astype(BF16)
    low_ref[...] = (scaled - high_ref[...].astype(F32)).astype(BF16)
    for i in range(q_ref.shape[1] // HD):
        a, b = i * HD, (i + 1) * HD
        score_ref[i] = lax.dot_general(
            jnp.concatenate([q_ref[:, a:b], q_ref[:, a:b]], 1), jnp.concatenate([high_ref[:, a:b], low_ref[:, a:b]], 1),
            (((1,), (1,)), ((), ())), preferred_element_type=F32,
        )


def finish_kernel(full_width, frames_ref, ctl_ref, score_ref, mine_ref, other_ref, sink_v_ref, came_v_ref, next_ref,
                  near_ref, far_ref, acc_ref, top_ref, den_ref, out_hbm, weight_ref, keep_ref, out_ref, sem):
    rows, cols = out_ref.shape
    span = 3 * FT
    factor = lax.rsqrt((mine_ref[...] + other_ref[...]) / full_width + EPSILON) * (1.0 / math.sqrt(HD))
    factor = jnp.broadcast_to(factor[:1, :span], (rows, span))
    heads = [(i, i * HD, (i + 1) * HD) for i in range(cols // HD)]
    sink = ctl_ref[:1, :1]
    window = ctl_ref[1:2, :1]
    here = lax.axis_index("tm")
    two = near_ref[FT:FT + 1, :1].astype(F32)
    has_last = jnp.where(jnp.full((1, 1), here, jnp.int32) > 0, window, 0.0)
    has_before = jnp.where((two < MISSING / 2) | (jnp.full((1, 1), here, jnp.int32) > 1), has_last, 0.0)
    slot = lax.broadcasted_iota(jnp.int32, (rows, span), 1)
    allow = jnp.where(slot < FT, has_last, jnp.where(slot < 2 * FT, has_before, sink))
    allowed = allow > 0.5
    live = lax.broadcasted_iota(jnp.int32, (rows, HD), 0) < frames_ref[0] * FT
    pick = jnp.broadcast_to(two, (FT, HD)) < MISSING / 2
    place = jnp.full((FT, HD), here, jnp.int32)
    second, even = place == 1, place % 2 == 0
    ones = jnp.ones((span, HD), BF16)
    for i, a, b in heads:
        score = jnp.where(allowed, score_ref[i] * factor, -jnp.inf)
        old = top_ref[:, a:b]
        top = jnp.maximum(old, jnp.max(score, axis=1, keepdims=True))
        keep_ref[i] = jnp.exp(old - top)
        weight_ref[i] = jnp.exp(score - top[:, :span]).astype(BF16)
    half = (len(heads) + 1) // 2
    copies = [
        pltpu.make_async_copy(out_ref.at[:, a:b], out_hbm.at[:, a:b], sem.at[n])
        for n, (a, b) in enumerate(((0, half * HD), (half * HD, cols))) if a < b
    ]
    for i, a, b in heads:
        c, d = cols + a, cols + b
        before = jnp.where(pick, near_ref[FT:, c:d], far_ref[:, c:d])
        first = jnp.where(second, next_ref[:, c:d], came_v_ref[:, a:b])
        first = jnp.where(even, sink_v_ref[:, a:b], first)
        vals = jnp.concatenate([near_ref[:FT, c:d], before, first], 0)
        both = jnp.dot(weight_ref[i], jnp.concatenate([vals, ones], 1), preferred_element_type=F32)
        keep = keep_ref[i]
        blended = (acc_ref[:, a:b] * keep + both[:, :HD]) * pl.reciprocal(den_ref[:, a:b] * keep + both[:, HD:])
        out_ref[:, a:b] = jnp.where(live, blended, 0.0).astype(BF16)
        if i == half - 1:
            copies[0].start()
    for copy in copies[1:]:
        copy.start()
    for copy in copies:
        copy.wait()


def local(queries, keys, values, q_gain, k_gain, frames, flags):
    rows, cols = queries.shape
    heads = lax.axis_size("head")
    full_width = cols * heads
    count = lax.axis_size("tm")
    here = lax.axis_index("tm")
    shape = jax.ShapeDtypeStruct
    block = shape((rows, cols), BF16)
    wide = shape((rows, cols), F32)
    frame = shape((FT, cols), BF16)
    swap = [(h, (h + 1) % heads) for h in range(heads)]
    in_hbm = lambda x: pltpu.with_memory_space_constraint(x, pltpu.HBM)
    scores = lambda n: [pltpu.VMEM((cols // HD, rows, n), F32), pltpu.VMEM((cols // HD, rows, n), BF16)]

    sink_k, sink_v, both = call(
        lead_kernel, (frame, frame, shape((FT, 2 * cols), BF16)), (in_hbm(keys), in_hbm(values)),
        specs=[HBM, HBM], scratch=[pltpu.SemaphoreType.DMA((2,))],
    )
    near, far = call(
        pack_kernel,
        (shape((2 * FT, 2 * cols), BF16), shape((FT, 2 * cols), BF16)),
        (frames, keys, values), specs=[SMEM, VMEM, VMEM],
    )
    near = lax.ppermute(near, "tm", [(i, i + 1) for i in range(count - 1)])
    far = lax.ppermute(far, "tm", [(i, i + 2) for i in range(count - 2)])
    both = lax.ppermute(both, "tm", [(0, 1)])
    rounds = tree_rounds(count)
    for number, (pairs, period) in enumerate(rounds):
        pairs = [pair for pair in pairs if pair != (0, 1)]
        came_k = lax.ppermute(sink_k, "tm", pairs)
        came_v = lax.ppermute(sink_v, "tm", pairs)
        if number < len(rounds) - 1:
            kept = here % period == 0
            sink_k = jnp.where(kept, sink_k, came_k)
            sink_v = jnp.where(kept, sink_v, came_v)
    mine = call(sums_kernel, shape((rows, LANES), F32), (queries, keys))
    other = lax.ppermute(mine, "head", swap)
    ctl, gains, qn, acc, top, den = call(
        lambda *refs: own_kernel(full_width, *refs),
        (shape((8, LANES), F32), shape((8, cols), F32), block, wide, wide, wide),
        (
            frames, in_hbm(flags), queries, keys, values, in_hbm(q_gain), in_hbm(k_gain), mine, other,
        ),
        specs=[SMEM, HBM, VMEM, VMEM, VMEM, HBM, HBM, VMEM, VMEM],
        scratch=[pltpu.VMEM((rows, cols), BF16)] + scores(rows) + [
            pltpu.VMEM((cols,), F32), pltpu.VMEM((cols,), F32), pltpu.SMEM((1, 2), jnp.int32),
            pltpu.SemaphoreType.DMA((3,)),
        ],
    )
    keys, mine = call(
        gather_kernel, (shape((3 * FT, cols), BF16), shape((8, LANES), F32)), (near, far, sink_k, came_k, both)
    )
    other = lax.ppermute(mine, "head", swap)
    score = call(
        score_kernel, shape((cols // HD, rows, 3 * FT), F32), (qn, keys, gains),
        scratch=[pltpu.VMEM((3 * FT, cols), BF16)] * 2,
    )
    return call(
        lambda *refs: finish_kernel(full_width, *refs), block,
        (frames, ctl, score, mine, other, sink_v, came_v, both, near, far, acc, top, den),
        specs=[SMEM] + [VMEM] * 12,
        scratch=[
            pltpu.VMEM((cols // HD, rows, 3 * FT), BF16), pltpu.VMEM((cols // HD, rows, HD), F32),
            pltpu.VMEM((rows, cols), BF16), pltpu.SemaphoreType.DMA((2,)),
        ],
        out_specs=HBM,
    )


def solution(mesh):
    placed = (
        P(("groups", "tm"), "head"),
        P(("groups", "tm"), "head"),
        P(("groups", "tm"), "head"),
        P("head"),
        P("head"),
        P(("groups", "tm")),
        P(("groups", "tm"), None),
    )
    return jax.shard_map(
        local, mesh=mesh, in_specs=placed, out_specs=P(("groups", "tm"), "head"), check_vma=False
    )
```
